32 devices in a mesh: term: 8 (over y, x, core), rep: 4 (over z).
Axes of the slice: x: 2, y: 2, z: 4, core: 2. Of those that a mesh axis runs over, the one named last changes fastest.
Arguments:
- panel_values: float32 [16, 8, 128, 128], P('rep', 'term'), may hold values from 0.01 to 0.3
- panel_ids: int32 [16, 8], P('rep', 'term'), may hold values from 0 to 1953, as said below
- block_rows: int32 [1792], P('term'), may hold values from 0 to 1953, as said below
- block_cols: int32 [1792], P('term'), may hold values from 0 to 1953, as said below
Outputs:
- blocks_out: float32 [1792, 128, 128], P(('term', 'rep'))
The draws below stay inside these ranges and needn't reach their ends.
Inputs may be any that keep to these rules, and one draw needn't show every extreme that they name: `panel_ids`: the 8 tile ids of one panel are distinct. For every output block b, some panel lists both block_rows[b] and block_cols[b]. For every output block b, some panel lists both block_rows[b] and block_cols[b].
All inputs are finite; a program needn't handle non-finite values.
Results may differ from the reference program's by a relative error of at most 0.0003.
Values sent between devices are 32-bit elements; how exact they have to be, the bound alone decides.
A program may use at most 192 MiB of HBM per device.

```python
import math
import jax
import jax.numpy as jnp
from jax import lax

VT = 1954
TILE = 128
PASS = 128
PANELS = 16
NZT = 8
HOTN = 16
HOT_PANEL = 6
NB = 1792


def pools(key):
    shuffled = (jax.random.permutation(jax.random.fold_in(key, 11), VT - 2) + 1).astype(jnp.int32)
    hot_pool = jnp.concatenate([jnp.array([0, VT - 1], jnp.int32), shuffled[:HOTN - 2]])
    cold_pool = shuffled[HOTN - 2:]
    return (hot_pool, cold_pool)


def pick_panel(key, panel, hot_pool, cold_pool):
    base = jax.random.fold_in(key, 1000 + panel)
    scores = jax.random.permutation(jax.random.fold_in(base, 1), HOTN).astype(jnp.int32)
    positions = jnp.arange(HOTN, dtype=jnp.int32)
    scores = jnp.where((panel == 0) & (positions < 2), positions - 2, scores)
    hot_pick = jnp.argsort(scores)[:HOT_PANEL]
    cold_pick = jax.random.permutation(jax.random.fold_in(base, 2), VT - HOTN)[:NZT - HOT_PANEL]
    chosen = jnp.concatenate([hot_pool[hot_pick], cold_pool[cold_pick]])
    mixing = jax.random.permutation(jax.random.fold_in(base, 3), NZT)
    return chosen[mixing]


def draw_panel_ids(key, part):
    hot_pool, cold_pool = pools(key)
    panels = jnp.arange(PANELS, dtype=jnp.int32)
    return jax.vmap(lambda panel: pick_panel(key, panel, hot_pool, cold_pool))(panels).astype(jnp.int32)


def block_pairs(key):
    table = draw_panel_ids(key, 0).reshape(PANELS * NZT)
    base = jax.random.fold_in(key, 21)
    chosen = jax.random.randint(jax.random.fold_in(base, 1), (NB,), 0, PANELS).astype(jnp.int32)
    slot_row = jax.random.randint(jax.random.fold_in(base, 2), (NB,), 0, NZT).astype(jnp.int32)
    slot_col = jax.random.randint(jax.random.fold_in(base, 3), (NB,), 0, NZT).astype(jnp.int32)
    rows = table[chosen * NZT + slot_row]
    cols = table[chosen * NZT + slot_col]
    rows = rows.at[0].set(0).at[1].set(VT - 1)
    cols = cols.at[0].set(VT - 1).at[1].set(0)
    return (rows.astype(jnp.int32), cols.astype(jnp.int32))


def draw_block_rows(key, part):
    return block_pairs(key)[0]


def draw_block_cols(key, part):
    return block_pairs(key)[1]


def block_scale(stream_key, extent, pieces, smallest, largest):
    factor_of, own = 1.0, jax.random.fold_in(stream_key, 6)
    for dim, parts in pieces:
        heights = jnp.exp(jax.random.uniform(jax.random.fold_in(own, dim), (parts,), jnp.float32, smallest / len(pieces), largest / len(pieces)))
        factor_of = factor_of * jnp.repeat(heights, extent[dim] // parts).reshape([-1 if axis == dim else 1 for axis in range(len(extent))])
    return factor_of


def setup_inputs(seed: int = 0) -> dict:
    arg_keys = jax.random.split(jax.random.key(seed), 5)
    panel_values = jnp.clip(jnp.exp(math.log(0.3) - 3.4011974 * jax.random.uniform(arg_keys[0], (PANELS, NZT, PASS, TILE), jnp.float32) ** block_scale(arg_keys[0], (PANELS, NZT, PASS, TILE), ((0, 4), (1, 8)), -0.2, 0.2)), 0.01, 0.3)
    panel_ids = draw_panel_ids(jax.random.fold_in(arg_keys[4], 71), 0)
    block_rows = draw_block_rows(jax.random.fold_in(arg_keys[4], 71), 0)
    block_cols = draw_block_cols(jax.random.fold_in(arg_keys[4], 71), 0)
    return {"panel_values": panel_values, "panel_ids": panel_ids, "block_rows": block_rows, "block_cols": block_cols}


def block_terms(tile_values, tile_ids, row_ids, col_ids):
    match_row = tile_ids[None, :] == row_ids[:, None]
    match_col = tile_ids[None, :] == col_ids[:, None]
    slot_row = jnp.argmax(match_row, axis=1).astype(jnp.int32)
    slot_col = jnp.argmax(match_col, axis=1).astype(jnp.int32)
    present = jnp.any(match_row, axis=1) & jnp.any(match_col, axis=1)
    left_tile = jnp.take(tile_values, slot_row, axis=0)
    right_tile = jnp.take(tile_values, slot_col, axis=0)
    product = jnp.einsum("gpi,gpj->gij", left_tile, right_tile, precision=lax.Precision.HIGHEST)
    return jnp.where(present[:, None, None], product, jnp.float32(0.0))


def reference(panel_values, panel_ids, block_rows, block_cols):
    width = math.gcd(NB, 256)
    rows_grouped = block_rows.reshape(NB // width, width)
    cols_grouped = block_cols.reshape(NB // width, width)

    def add_panel(total, panel):
        tile_values, tile_ids = panel

        def one_group(pair):
            return block_terms(tile_values, tile_ids, pair[0], pair[1])

        terms = lax.map(one_group, (rows_grouped, cols_grouped))
        return total + terms.reshape(NB, TILE, TILE), None

    start = jnp.zeros((NB, TILE, TILE), jnp.float32)
    total, _ = lax.scan(add_panel, start, (panel_values, panel_ids))
    return total
```

```python
import functools

import jax
import jax.numpy as jnp
from jax import lax
from jax.experimental import pallas as pl
from jax.experimental.pallas import tpu as pltpu
from jax.sharding import PartitionSpec as P

MESH = pl.DeviceIdType.MESH
CORES = 2
SIDE = 2
ROWS = 8
LANES = 128
DEPTH = 4
EACH = 4
UNROLL = 6
WINDOW = 3
LEVELS = {True: (0, 1, 2), False: (1, 0, 2)}
T_LINK, T_HOP, T_CROSS, T_OP, T_SETTLE = 1.43, 2.2, 1.0, 0.03, 4.0
T_GRAM, T_COLLECT, T_LIST, T_TURN = 0.66, 0.65, 0.5, 1.0
X, Y, C, IN, OUT = range(5)
FLIP_X = {"S": "X", "X": "S", "Y": "D", "D": "Y"}
FLIP_Y = {"S": "Y", "Y": "S", "X": "D", "D": "X"}
COLUMNS = ("S", "X", "Y", "D")


def link_orders(end):
    own, every = (0, range(EACH)) if end else (1, range(EACH))
    whole = lambda column, level: [(column, level, j) for j in every]

    def crossing(levels, rest, odd, other):
        order = []
        for level in levels:
            for j in range(0, EACH, 2):
                order += [("S", level, j), ("S", level, j + 1), (other, level, j + odd)]
        for level in rest:
            order += whole("S", level)
        return order

    if end:
        return {
            X: crossing((0, 1), (2, 3), 0, "Y"),
            Y: crossing((0, 1), (2, 3), 1, "X"),
            IN: whole("S", 0) + whole("D", 0),
        }
    return {
        X: crossing((1,), (0, 2, 3), 0, "Y"),
        Y: crossing((1,), (0, 2, 3), 1, "X"),
        IN: whole("S", 1) + whole("D", 1) + whole("S", 0) + whole("D", 0),
        OUT: whole("S", 1) + whole("S", 2) + whole("D", 2) + whole("S", 3) + whole("D", 3),
    }


def play_orders():
    orders = {end: link_orders(end) for end in (True, False)}
    into = {
        (True, X): (True, lambda c: (FLIP_X[c[0]], c[1], c[2])),
        (True, Y): (True, lambda c: (FLIP_Y[c[0]], c[1], c[2])),
        (True, IN): (False, lambda c: c),
        (False, X): (False, lambda c: (FLIP_X[c[0]], c[1], c[2])),
        (False, Y): (False, lambda c: (FLIP_Y[c[0]], c[1], c[2])),
        (False, IN): (False, lambda c: (c[0], DEPTH - 1 - c[1], c[2])),
        (False, OUT): (True, lambda c: c),
    }
    works = {}
    for end in (True, False):
        todo = []
        for level in LEVELS[end]:
            for half in range(0, EACH, 2):
                todo += [(T_GRAM, level, half), (T_GRAM, level, half + 1), (T_COLLECT, None, 0), (T_COLLECT, None, 0)]
        works[end] = todo + [(T_LIST, DEPTH - 1, 0), (T_TURN, None, 0), (T_TURN, None, 0)]
    clock = {True: 0.0, False: 0.0}
    have = {end: {("S", 0 if end else 1, j) for j in range(EACH)} for end in (True, False)}
    coming = {True: [], False: []}
    across = {True: {}, False: {}}
    crossed = {True: set(), False: set()}
    crossing = {True: [], False: []}
    flight = {key: [] for key in into}
    sent = {key: set() for key in into}
    free = {key: 0.0 for key in into}
    worked = {True: 0, False: 0}
    ops = {True: [], False: []}

    def cross(end, chunk):
        ops[end].append(("start", C, chunk))
        crossing[end].append((clock[end] + T_SETTLE, chunk))
        across[end][chunk] = clock[end] + T_CROSS

    def act(end):
        now = clock[end]
        for arrival in sorted(coming[end]):
            if arrival[0] <= now:
                coming[end].remove(arrival)
                have[end].add(arrival[1])
                ops[end].append(("take", None, arrival[1]))
                cross(end, arrival[1])
                return T_OP
        for way, order in orders[end].items():
            key = (end, way)
            full = len(flight[key]) == WINDOW
            ready = [chunk for chunk in order if chunk in have[end] and chunk not in sent[key]]
            if ready and not (full and flight[key][0][0] > now):
                chunk = ready[0]
                if full:
                    ops[end].append(("settle", way, flight[key].pop(0)[1]))
                ops[end].append(("start", way, chunk))
                sent[key].add(chunk)
                free[key] = max(free[key], now) + T_LINK
                flight[key].append((free[key], chunk))
                receiver, rename = into[key]
                coming[receiver].append((free[key] + T_HOP, rename(chunk)))
                return T_OP
        if worked[end] < len(works[end]):
            lasts, level, j = works[end][worked[end]]
            needed = [(column, level, j) for column in COLUMNS] if level is not None else []
            if all(c in have[end] and across[end].get(c, now + 1) <= now for c in needed):
                while crossing[end] and crossing[end][0][0] <= now:
                    ops[end].append(("settle", C, crossing[end].pop(0)[1]))
                ops[end] += [("across", None, c) for c in needed if c not in crossed[end]]
                crossed[end].update(needed)
                ops[end].append(("work", None, None))
                worked[end] += 1
                return lasts
        return None

    for end in (True, False):
        for j in range(EACH):
            cross(end, ("S", 0 if end else 1, j))
    while True:
        end = clock[True] <= clock[False]
        spent = act(end)
        if spent is not None:
            clock[end] += spent
            continue
        later = [t for t, _ in coming[end]] + list(across[end].values())
        later += [held[0][0] for (kind, _), held in flight.items() if kind == end and held]
        later = [t for t in later if t > clock[end]]
        other = clock[not end]
        if not later and act(not end) is None and not [t for t, _ in coming[not end] if t > other]:
            break
        clock[end] = min(later + [max(other, clock[end]) + T_OP])
    for end in (True, False):
        for (kind, way), held in flight.items():
            if kind == end:
                ops[end] += [("settle", way, chunk) for _, chunk in held]
        ops[end] += [("settle", C, chunk) for _, chunk in crossing[end]]
        every = [(column, level, j) for column in COLUMNS for level in range(DEPTH) for j in range(EACH)]
        ops[end] += [("across", None, c) for c in every if c not in crossed[end]]
    return ops, clock


def gather_kernel(
    blocks, ids_hbm, rows_hbm, cols_hbm, shard_ref, tiles_ref, total_ref, list_ref, ids_in, rows_in, cols_in,
    turned_ref, gram0_ref, gram1_ref, left_ref, right_ref, table_ref, index_ref,
    small_sem, own_sem, table_sem, send_sem, recv_sem,
):
    term = lax.axis_index("term")
    z = lax.axis_index("rep")
    core = term % CORES
    x = (term // CORES) % SIDE
    y = term // (CORES * SIDE)
    terms = CORES * SIDE * SIDE
    upper = (z >= DEPTH // 2).astype(jnp.int32)
    at_end = (z == 0) | (z == DEPTH - 1)
    inner = jnp.logical_not(at_end)
    inward = 1 - 2 * upper
    size = shard_ref.shape[1]

    def term_of(column, at_core):
        at_x = 1 - x if column in ("X", "D") else x
        at_y = 1 - y if column in ("Y", "D") else y
        return (at_y * SIDE + at_x) * CORES + at_core

    def level_of(level):
        return level + upper * (DEPTH - 1 - 2 * level)

    def slot_of(column, level, at_core):
        return level_of(level) * terms + term_of(column, at_core)

    target = {
        X: (term_of("X", core), z),
        Y: (term_of("Y", core), z),
        C: (term_of("S", 1 - core), z),
        IN: (term, z + inward),
        OUT: (term, z - inward),
    }
    smalls = [
        pltpu.make_async_copy(source, held, small_sem.at[i])
        for i, (source, held) in enumerate(((ids_hbm, ids_in), (rows_hbm, rows_in), (cols_hbm, cols_in)))
    ]
    for small in smalls:
        small.start()
    barrier = pltpu.get_barrier_semaphore()

    def greet(way):
        pl.semaphore_signal(barrier, inc=1, device_id=target[way], device_id_type=MESH)

    for way in (X, Y, C, IN):
        greet(way)
    pl.when(inner)(lambda: greet(OUT))
    own_slot = z * terms + term
    own = pltpu.make_async_copy(shard_ref, tiles_ref.at[own_slot, pl.ds(ROWS, EACH * size)], own_sem)
    own.start()
    sub = lax.broadcasted_iota(jnp.int32, (ROWS, LANES), 0)
    lane = lax.broadcasted_iota(jnp.int32, (ROWS, LANES), 1)
    ids = jnp.full((ROWS, LANES), -1, jnp.int32)
    for small in smalls:
        small.wait()
    for j in range(EACH):
        ids = jnp.where(sub == j, ids_in[j], ids)
    tiles_ref[own_slot, :ROWS] = ids.astype(jnp.float32)
    own.wait()
    pl.semaphore_wait(barrier, 4 + inner.astype(jnp.int32))

    def rows_of(j):
        return pl.ds(0, ROWS + size) if j == 0 else pl.ds(ROWS + j * size, size)

    def part(slot, j):
        return tiles_ref.at[slot, rows_of(j)]

    def copy(way, chunk):
        column, level, j = chunk
        slot = slot_of(column, level, core)
        return pltpu.make_async_remote_copy(
            src_ref=part(slot, j), dst_ref=part(slot, j),
            send_sem=send_sem.at[way, level * DEPTH + COLUMNS.index(column), j],
            recv_sem=recv_sem.at[slot, j], device_id=target[way], device_id_type=MESH,
        )

    def arrived(chunk, at_core):
        column, level, j = chunk
        slot = slot_of(column, level, at_core)
        pltpu.make_async_remote_copy(
            src_ref=part(slot, j), dst_ref=part(slot, j), send_sem=send_sem.at[0, 0, 0],
            recv_sem=recv_sem.at[slot, j], device_id=target[C], device_id_type=MESH,
        ).wait_recv()

    ops, _ = play_orders()
    groups = {}
    for end in (True, False):
        groups[end] = [[]]
        for op in ops[end]:
            if op[0] == "work":
                groups[end].append([])
            else:
                groups[end][-1].append(op)

    def play(end, index):
        for name, way, chunk in groups[end][index]:
            if name == "take":
                arrived(chunk, core)
            elif name == "across":
                arrived(chunk, 1 - core)
            elif name == "start":
                copy(way, chunk).start()
            else:
                copy(way, chunk).wait_send()

    def both_kinds(act):
        pl.when(at_end)(lambda: act(True))
        pl.when(inner)(lambda: act(False))

    halves = EACH // 2
    pairs = (DEPTH - 1) * halves

    wanted_row = jnp.full((ROWS, LANES), -2, jnp.int32)
    wanted_col = wanted_row
    for b in range(blocks):
        wanted_row = jnp.where(lane == b, rows_in[z * blocks + b], wanted_row)
        wanted_col = jnp.where(lane == b, cols_in[z * blocks + b], wanted_col)
    table_ref[0] = wanted_row
    table_ref[1] = wanted_col

    def clear(b, _):
        total_ref[b] = jnp.zeros((size, size), jnp.float32)
        turned_ref[b] = jnp.zeros((size, size), jnp.float32)
        return 0

    lax.fori_loop(0, blocks, clear, 0)
    gram0_ref[terms * terms] = jnp.zeros((size, size), jnp.float32)
    gram1_ref[terms * terms] = jnp.zeros((size, size), jnp.float32)

    def slots_at(level):
        want_row, want_col = table_ref[0].astype(jnp.float32), table_ref[1].astype(jnp.float32)
        slot_row = jnp.full((ROWS, LANES), -1, jnp.int32)
        slot_col = slot_row
        for t in range(terms):
            listed = tiles_ref[level * terms + t, :ROWS]
            slot_row = jnp.where(listed == want_row, t, slot_row)
            slot_col = jnp.where(listed == want_col, t, slot_col)
        return slot_row, slot_col, (slot_row >= 0) & (slot_col >= 0)

    table_copy = pltpu.make_async_copy(table_ref.at[pl.ds(2, 2)], index_ref, table_sem)

    def make_table(level):
        slot_row, slot_col, present = slots_at(level)
        table_ref[2] = jnp.where(present, slot_row * terms + slot_col, terms * terms)
        table_ref[3] = jnp.where(present, slot_col * terms + slot_row, terms * terms)
        table_copy.start()

    def gram(level, j, side, gram_ref):
        for t in range(terms):
            value = tiles_ref[level * terms + t, pl.ds(pl.multiple_of(ROWS + j * size, ROWS), size)]
            high = value.astype(jnp.bfloat16)
            low = (value - high.astype(jnp.float32)).astype(jnp.bfloat16)
            here = pl.ds(t * size, size)
            right_ref[side, :size, here] = high * jnp.bfloat16(0.5)
            right_ref[side, size:, here] = low
            left_ref[side, here, :size] = high.T
            left_ref[side, here, size:] = high.T
        for r in range(terms):
            value = jnp.dot(
                left_ref[side, r * size : (r + 1) * size], right_ref[side], preferred_element_type=jnp.float32
            )
            for c in range(terms):
                gram_ref[r * terms + c] = value[:, c * size : (c + 1) * size]

    def collect(half, part):
        def one(b, _):
            j = half * 2
            total_ref[b] = total_ref[b] + (gram0_ref[index_ref[0, j, b]] + gram1_ref[index_ref[0, j + 1, b]])
            turned_ref[b] = turned_ref[b] + (gram0_ref[index_ref[1, j, b]] + gram1_ref[index_ref[1, j + 1, b]])
            return 0

        lax.fori_loop(part * (blocks // 2), (part + 1) * (blocks // 2), one, 0, unroll=4)

    def transfers(k, step):
        for at in range(pairs):
            pl.when(k == at)(lambda: both_kinds(lambda end: play(end, at * 4 + step)))

    def pair(k, _):
        half = k % halves
        near = k // halves
        level = level_of(jnp.where(at_end | (near == 2), near, 1 - near))
        transfers(k, 0)
        pl.when(half == 0)(lambda: make_table(level))
        gram(level, half * 2, 0, gram0_ref)
        transfers(k, 1)
        gram(level, half * 2 + 1, 1, gram1_ref)
        transfers(k, 2)
        pl.when(half == 0)(lambda: table_copy.wait())
        collect(half, 0)
        transfers(k, 3)
        collect(half, 1)
        return 0

    lax.fori_loop(0, pairs, pair, 0)

    final_level = DEPTH - 1

    both_kinds(lambda end: play(end, pairs * 4))
    slot_row, slot_col, present = slots_at(level_of(final_level))
    before = (
        lax.broadcasted_iota(jnp.int32, (LANES, LANES), 0) < lax.broadcasted_iota(jnp.int32, (LANES, LANES), 1)
    ).astype(jnp.float32)
    code = (lane * terms + slot_row) * terms + slot_col
    ones = jnp.where(present, 1.0, 0.0).astype(jnp.float32)
    ahead = jnp.dot(ones, before, preferred_element_type=jnp.float32)
    place = jnp.where(present, ahead, float(LANES)).astype(jnp.int32)
    count = jnp.sum(jnp.where(present, 1, 0), axis=1, keepdims=True)
    entries = jnp.where(lane == LANES - 1, count, jnp.where(lane >= count, blocks * terms * terms, 0))
    for b in range(blocks):
        entries = entries + jnp.where(place[:, b : b + 1] == lane, code[:, b : b + 1], 0)
    list_ref[...] = entries

    def turn(i, _):
        for k in range(4):
            b = i * 4 + k
            total_ref[b] = total_ref[b] + turned_ref[b].T
        return 0

    both_kinds(lambda end: play(end, pairs * 4 + 1))
    lax.fori_loop(0, blocks // 8, turn, 0)
    both_kinds(lambda end: play(end, pairs * 4 + 2))
    lax.fori_loop(blocks // 8, blocks // 4, turn, 0)
    both_kinds(lambda end: play(end, pairs * 4 + 3))


def gather_by_hand(ids, rows, cols, shard, blocks):
    terms = CORES * SIDE * SIDE
    size = shard.shape[1]
    vmem = pl.BlockSpec(memory_space=pltpu.VMEM)
    return pl.pallas_call(
        functools.partial(gather_kernel, blocks),
        out_shape=(
            pltpu.VMEM((DEPTH * terms, ROWS + shard.shape[0], size), jnp.float32),
            pltpu.VMEM((blocks + 1, size, size), jnp.float32),
            pltpu.VMEM((ROWS, LANES), jnp.int32),
        ),
        in_specs=[pl.BlockSpec(memory_space=pltpu.HBM)] * 4,
        out_specs=(vmem, vmem, vmem),
        scratch_shapes=[
            pltpu.SMEM(ids.shape, jnp.int32),
            pltpu.SMEM(rows.shape, jnp.int32),
            pltpu.SMEM(cols.shape, jnp.int32),
            pltpu.VMEM((blocks, size, size), jnp.float32),
            pltpu.VMEM((terms * terms + 1, size, size), jnp.float32),
            pltpu.VMEM((terms * terms + 1, size, size), jnp.float32),
            pltpu.VMEM((2, terms * size, 2 * size), jnp.bfloat16),
            pltpu.VMEM((2, 2 * size, terms * size), jnp.bfloat16),
            pltpu.VMEM((4, ROWS, LANES), jnp.int32),
            pltpu.SMEM((2, ROWS, LANES), jnp.int32),
            pltpu.SemaphoreType.DMA((3,)),
            pltpu.SemaphoreType.DMA,
            pltpu.SemaphoreType.DMA,
            pltpu.SemaphoreType.DMA((5, DEPTH * len(COLUMNS), EACH)),
            pltpu.SemaphoreType.DMA((DEPTH * terms, EACH)),
        ],
        compiler_params=pltpu.CompilerParams(
            collective_id=0, has_side_effects=True, vmem_limit_bytes=30 * 1024 * 1024
        ),
    )(*(pltpu.with_memory_space_constraint(value, pltpu.HBM) for value in (ids, rows, cols, shard)))


def split(value):
    high = value.astype(jnp.bfloat16)
    return high, (value - high.astype(jnp.float32)).astype(jnp.bfloat16)


def prepare(value, s, left_ref, right_ref):
    size = value.shape[0]
    high, low = split(value)
    right_ref[s, :size] = high
    right_ref[s, size : 2 * size] = high
    right_ref[s, 2 * size :] = low
    high, low = split(value.T)
    left_ref[s, :, :size] = high
    left_ref[s, :, size : 2 * size] = low
    left_ref[s, :, 2 * size :] = high


def add_products(slots, read, count, out_ref, left_ref, right_ref, filled):
    def entries(first, width):
        picked = []
        for k in range(width):
            code = read(first + k)
            pair = code % (slots * slots)
            picked.append((code // (slots * slots), pair // slots, pair % slots))
        sums = [
            out_ref[b] + jnp.dot(left_ref[r], right_ref[c], preferred_element_type=jnp.float32)
            for b, r, c in picked
        ]
        for (b, _, _), value in zip(picked, sums):
            out_ref[b] = value

    groups = (count + UNROLL - 1) // UNROLL if filled else count // UNROLL
    pl.loop(0, groups)(lambda i: entries(i * UNROLL, UNROLL))
    if filled:
        return
    pl.loop(groups * UNROLL, count)(lambda i: entries(i, 1))


def clear(out_ref):
    def one(b, _):
        out_ref[b] = jnp.zeros(out_ref.shape[1:], jnp.float32)
        return 0

    lax.fori_loop(0, out_ref.shape[0], one, 0)


def held_kernel(blocks, tiles_ref, total_in, list_in, out_ref, total_ref, left_ref, right_ref, list_ref, list_sem, out_sem):
    terms = CORES * SIDE * SIDE
    size = tiles_ref.shape[2]
    z = lax.axis_index("rep")
    last = jnp.where(z >= DEPTH // 2, 0, DEPTH - 1) * terms
    fetch = pltpu.make_async_copy(list_in, list_ref, list_sem)
    fetch.start()

    def panel(j):
        row = pl.multiple_of(ROWS + j * size, ROWS)
        for s in range(terms):
            prepare(tiles_ref[last + s, pl.ds(row, size)], s, left_ref, right_ref)
        pl.when(j == 0)(lambda: fetch.wait())
        add_products(terms, lambda k: list_ref[j, k], list_ref[j, LANES - 1], total_ref, left_ref, right_ref, True)

    pl.loop(0, EACH)(panel)
    pieces = out_sem.shape[0]
    each = blocks // pieces
    outs = [
        pltpu.make_async_copy(total_ref.at[pl.ds(i * each, each)], out_ref.at[pl.ds(i * each, each)], out_sem.at[i])
        for i in range(pieces)
    ]
    for out in outs:
        out.start()
    for out in outs:
        out.wait()


def held_products(tiles, total, entries, blocks):
    size = tiles.shape[2]
    terms = CORES * SIDE * SIDE
    pieces = next(n for n in (8, 7, 4, 2, 1) if blocks % n == 0)
    vmem = pl.BlockSpec(memory_space=pltpu.VMEM)
    return pl.pallas_call(
        functools.partial(held_kernel, blocks),
        out_shape=(
            jax.ShapeDtypeStruct((blocks, size, size), jnp.float32),
            pltpu.VMEM(total.shape, jnp.float32),
        ),
        in_specs=[vmem, vmem, vmem],
        out_specs=(pl.BlockSpec(memory_space=pl.ANY), vmem),
        input_output_aliases={1: 1},
        scratch_shapes=[
            pltpu.VMEM((terms, size, 3 * size), jnp.bfloat16),
            pltpu.VMEM((terms, 3 * size, size), jnp.bfloat16),
            pltpu.SMEM((ROWS, LANES), jnp.int32),
            pltpu.SemaphoreType.DMA,
            pltpu.SemaphoreType.DMA((pieces,)),
        ],
        compiler_params=pltpu.CompilerParams(vmem_limit_bytes=16 * 1024 * 1024),
    )(tiles, total, entries)[0]


def product_kernel(slots, base, count_ref, list_ref, tiles_ref, out_ref, left_ref, right_ref):
    panel = pl.program_id(0)

    pl.when(panel == 0)(lambda: clear(out_ref))
    pl.loop(0, slots)(lambda s: prepare(tiles_ref[0, s], s, left_ref, right_ref))
    add_products(
        slots, lambda k: list_ref[panel * base + k], count_ref[panel], out_ref, left_ref, right_ref, False
    )


def products(tiles, slots, panels_each, counts, entries, blocks):
    groups, size = tiles.shape[0], tiles.shape[3]
    return pl.pallas_call(
        functools.partial(product_kernel, slots, entries.shape[1]),
        out_shape=jax.ShapeDtypeStruct((blocks, size, size), jnp.float32),
        grid_spec=pltpu.PrefetchScalarGridSpec(
            num_scalar_prefetch=2,
            grid=(groups * panels_each,),
            in_specs=[
                pl.BlockSpec(
                    (1, slots, size, size), lambda p, *_: (p // panels_each, 0, p % panels_each, 0)
                )
            ],
            out_specs=pl.BlockSpec((blocks, size, size), lambda p, *_: (0, 0, 0)),
            scratch_shapes=[
                pltpu.VMEM((slots, size, 3 * size), jnp.bfloat16),
                pltpu.VMEM((slots, 3 * size, size), jnp.bfloat16),
            ],
        ),
        compiler_params=pltpu.CompilerParams(
            dimension_semantics=("arbitrary",), vmem_limit_bytes=56 * 1024 * 1024
        ),
    )(counts, entries.reshape(-1), tiles)


def block_list(ids, rows, cols):
    slots, blocks = ids.shape[1], rows.shape[0]
    order = jnp.arange(slots, dtype=jnp.int32)[None, :, None]
    match_row = ids[:, :, None] == rows[None, None, :]
    match_col = ids[:, :, None] == cols[None, None, :]
    slot_row = jnp.sum(jnp.where(match_row, order, 0), axis=1)
    slot_col = jnp.sum(jnp.where(match_col, order, 0), axis=1)
    present = jnp.any(match_row, axis=1) & jnp.any(match_col, axis=1)
    number = jnp.arange(blocks, dtype=jnp.int32)
    code = (number[None, :] * slots + slot_row) * slots + slot_col
    ahead = jnp.sum(
        jnp.where(present[:, None, :] & (number[None, None, :] < number[None, :, None]), 1, 0), axis=2
    )
    chosen = present[:, None, :] & (ahead[:, None, :] == number[None, :, None])
    entries = jnp.sum(jnp.where(chosen, code[:, None, :], 0), axis=2)
    counts = jnp.sum(present.astype(jnp.int32), axis=1)
    return counts.astype(jnp.int32), entries.astype(jnp.int32)


def solution(mesh):
    depth, terms = mesh.shape["rep"], mesh.shape["term"]

    def by_hand(panel_values, panel_ids, rows, cols, blocks):
        panels_each, _, passages, size = panel_values.shape
        tiles, total, entries = gather_by_hand(
            panel_ids.reshape(panels_each), rows, cols, panel_values.reshape(panels_each * passages, size), blocks
        )
        return held_products(tiles, total, entries, blocks)

    def local(panel_values, panel_ids, block_rows, block_cols):
        panels_each, own_slots, passages, size = panel_values.shape
        blocks = block_rows.shape[0] // depth
        slots = terms * own_slots
        shaped = own_slots == 1 and panels_each == EACH and passages == size == LANES
        if terms == CORES * SIDE * SIDE and depth == DEPTH and shaped and blocks + UNROLL < LANES and blocks % 4 == 0:
            return by_hand(panel_values, panel_ids, block_rows, block_cols, blocks)
        first = lax.axis_index("rep") * blocks
        rows = lax.dynamic_slice_in_dim(block_rows, first, blocks)
        cols = lax.dynamic_slice_in_dim(block_cols, first, blocks)
        shard = jnp.swapaxes(panel_values, 0, 1).reshape(own_slots, panels_each * passages, size)
        tiles = lax.all_gather(shard, ("rep", "term"), axis=0, tiled=True)
        tiles = tiles.reshape(depth, slots, panels_each * passages, size)
        ids = lax.all_gather(panel_ids.T, ("rep", "term"), axis=0, tiled=True)
        ids = ids.reshape(depth, slots, panels_each)
        ids = jnp.swapaxes(ids, 1, 2).reshape(depth * panels_each, slots)
        counts, entries = block_list(ids, rows, cols)
        return products(tiles, slots, panels_each, counts, entries, blocks)

    placed = (P("rep", "term", None, None), P("rep", "term"), P("term"), P("term"))
    return jax.shard_map(
        local, mesh=mesh, in_specs=placed, out_specs=P(("term", "rep"), None, None), check_vma=False
    )
```

```python
import functools

import jax
import jax.numpy as jnp
from jax import lax
from jax.experimental import pallas as pl
from jax.experimental.pallas import tpu as pltpu
from jax.sharding import PartitionSpec as P

MESH = pl.DeviceIdType.MESH
CORES = 2
SIDE = 2
ROWS = 8
LANES = 128
DEPTH = 4
EACH = 4
UNROLL = 6
WINDOW = 2
LEVELS = {True: (0, 1, 2, 3), False: (1, 0, 2, 3)}
PAIRS = DEPTH * EACH // 2
KEPT = 32
BATCH = 16
LATE_BATCH = 10
T_LINK, T_HOP, T_CROSS, T_OP = 1.46, 2.2, 1.1, 0.08
T_SETUP, T_PREPARE, T_PRODUCTS, T_COLLECT = 1.0, 0.7, 0.5, 0.6
X, Y, C, IN, OUT = range(5)
FLIP_X = {"S": "X", "X": "S", "Y": "D", "D": "Y"}
FLIP_Y = {"S": "Y", "Y": "S", "X": "D", "D": "X"}
COLUMNS = ("S", "X", "Y", "D")


def link_orders(end):
    own, every = (0, range(EACH)) if end else (1, range(EACH))
    whole = lambda column, level: [(column, level, j) for j in every]

    def crossing(levels, rest, odd, other):
        order = []
        for level in levels:
            order += [(other, level, odd), (other, level, 2 + odd)]
            order += [("S", level, j + 1 - odd - 2 * (j % 2) * (1 - odd)) for j in every]
        for level in rest:
            order += whole("S", level)
        return order

    if end:
        return {
            X: crossing((0, 1), (2, 3), 0, "Y"),
            Y: crossing((0, 1), (2, 3), 1, "X"),
            IN: whole("S", 0) + whole("D", 0),
        }
    return {
        X: crossing((1,), (0, 2, 3), 0, "Y"),
        Y: crossing((1,), (0, 2, 3), 1, "X"),
        IN: whole("S", 1) + whole("D", 1) + whole("S", 0) + whole("D", 0),
        OUT: whole("S", 1) + whole("S", 2) + whole("D", 2) + whole("S", 3) + whole("D", 3),
    }


def play_orders():
    orders = {end: link_orders(end) for end in (True, False)}
    into = {
        (True, X): (True, lambda c: (FLIP_X[c[0]], c[1], c[2])),
        (True, Y): (True, lambda c: (FLIP_Y[c[0]], c[1], c[2])),
        (True, IN): (False, lambda c: c),
        (False, X): (False, lambda c: (FLIP_X[c[0]], c[1], c[2])),
        (False, Y): (False, lambda c: (FLIP_Y[c[0]], c[1], c[2])),
        (False, IN): (False, lambda c: (c[0], DEPTH - 1 - c[1], c[2])),
        (False, OUT): (True, lambda c: c),
    }
    works = {}
    for end in (True, False):
        pairs = [(level, half) for level in LEVELS[end] for half in range(EACH // 2)][: PAIRS - 1]
        works[end] = [(T_SETUP, [])]
        for level, half in pairs:
            needed = [(column, level, half) for column in COLUMNS]
            works[end] += [(T_PREPARE, needed), (T_PRODUCTS, []), (T_PRODUCTS, []), (T_COLLECT, [])]
    clock = {True: 0.0, False: 0.0}
    have = {end: {("S", 0 if end else 1, j) for j in range(EACH)} for end in (True, False)}
    coming = {True: [], False: []}
    across = {True: {}, False: {}}
    crossed = {True: set(), False: set()}
    flight = {key: [] for key in into}
    sent = {key: set() for key in into}
    free = {key: 0.0 for key in into}
    worked = {True: 0, False: 0}
    ops = {True: [], False: []}

    def cross(end, column, level, half):
        ops[end].append(("cross", None, (column, level, half)))
        across[end][column, level, half] = clock[end] + T_CROSS

    def act(end):
        now = clock[end]
        for arrival in sorted(coming[end]):
            if arrival[0] <= now:
                column, level, j = arrival[1]
                coming[end].remove(arrival)
                have[end].add(arrival[1])
                ops[end].append(("take", None, arrival[1]))
                if (column, level, j ^ 1) in have[end]:
                    cross(end, column, level, j // 2)
                return T_OP
        for way, order in orders[end].items():
            key = (end, way)
            while flight[key] and flight[key][0] <= now:
                flight[key].pop(0)
            ready = [chunk for chunk in order if chunk in have[end] and chunk not in sent[key]]
            if ready and len(flight[key]) < WINDOW:
                chunk = ready[0]
                ops[end].append(("start", way, chunk))
                sent[key].add(chunk)
                free[key] = max(free[key], now) + T_LINK
                flight[key].append(free[key])
                receiver, rename = into[key]
                coming[receiver].append((free[key] + T_HOP, rename(chunk)))
                return T_OP
        if worked[end] < len(works[end]):
            lasts, needed = works[end][worked[end]]
            if all(across[end].get(c, now + 1) <= now for c in needed):
                ops[end] += [("across", None, c) for c in needed]
                crossed[end].update(needed)
                ops[end].append(("work", None, None))
                worked[end] += 1
                return lasts
        return None

    for end in (True, False):
        for half in range(EACH // 2):
            cross(end, "S", 0 if end else 1, half)
    while True:
        end = clock[True] <= clock[False]
        spent = act(end)
        if spent is not None:
            clock[end] += spent
            continue
        later = [t for t, _ in coming[end]] + list(across[end].values())
        later += [held[0] for (kind, _), held in flight.items() if kind == end and held]
        later = [t for t in later if t > clock[end]]
        other = clock[not end]
        if not later and act(not end) is None and not [t for t, _ in coming[not end] if t > other]:
            break
        clock[end] = min(later + [max(other, clock[end]) + T_OP])
    for end in (True, False):
        every = [(column, level, half) for column in COLUMNS for level in range(DEPTH) for half in range(EACH // 2)]
        ops[end] += [("across", None, c) for c in every if c not in crossed[end]]
        for way, order in orders[end].items():
            for column, level in dict.fromkeys((chunk[0], chunk[1]) for chunk in order):
                panels = [j for c, l, j in order if (c, l) == (column, level)]
                ops[end].append(("settle", way, (column, level, panels)))
        ops[end] += [("settle", C, (column, level, list(range(EACH)))) for column in COLUMNS for level in range(DEPTH)]
    return ops, clock


def gather_kernel(
    blocks, ids_hbm, rows_hbm, cols_hbm, shard_ref, tiles_ref, total_ref, list_ref, ids_in, rows_in, cols_in,
    made_ref, left_ref, right_ref, table_ref, index_ref,
    small_sem, own_sem, table_sem, send_sem, recv_sem, cross_sem,
):
    term = lax.axis_index("term")
    z = lax.axis_index("rep")
    core = term % CORES
    x = (term // CORES) % SIDE
    y = term // (CORES * SIDE)
    terms = CORES * SIDE * SIDE
    upper = (z >= DEPTH // 2).astype(jnp.int32)
    at_end = (z == 0) | (z == DEPTH - 1)
    inner = jnp.logical_not(at_end)
    inward = 1 - 2 * upper
    size = shard_ref.shape[1]

    def term_of(column, at_core):
        at_x = 1 - x if column in ("X", "D") else x
        at_y = 1 - y if column in ("Y", "D") else y
        return (at_y * SIDE + at_x) * CORES + at_core

    def level_of(level):
        return level + upper * (DEPTH - 1 - 2 * level)

    def slot_of(column, level, at_core):
        return level_of(level) * terms + term_of(column, at_core)

    target = {
        X: (term_of("X", core), z),
        Y: (term_of("Y", core), z),
        C: (term_of("S", 1 - core), z),
        IN: (term, z + inward),
        OUT: (term, z - inward),
    }
    smalls = [
        pltpu.make_async_copy(source, held, small_sem.at[i])
        for i, (source, held) in enumerate(((ids_hbm, ids_in), (rows_hbm, rows_in), (cols_hbm, cols_in)))
    ]
    for small in smalls:
        small.start()
    barrier = pltpu.get_barrier_semaphore()

    def greet(way):
        pl.semaphore_signal(barrier, inc=1, device_id=target[way], device_id_type=MESH)

    for way in (X, Y, C, IN):
        greet(way)
    pl.when(inner)(lambda: greet(OUT))
    own_slot = z * terms + term
    own = pltpu.make_async_copy(shard_ref, tiles_ref.at[own_slot, pl.ds(ROWS, EACH * size)], own_sem)
    own.start()
    sub = lax.broadcasted_iota(jnp.int32, (ROWS, LANES), 0)
    lane = lax.broadcasted_iota(jnp.int32, (ROWS, LANES), 1)
    ids = jnp.full((ROWS, LANES), -1, jnp.int32)
    for small in smalls:
        small.wait()
    for j in range(EACH):
        ids = jnp.where(sub == j, ids_in[j], ids)
    tiles_ref[own_slot, :ROWS] = ids.astype(jnp.float32)
    own.wait()
    pl.semaphore_wait(barrier, 4 + inner.astype(jnp.int32))

    def rows_of(j, width=1):
        return pl.ds(0, ROWS + width * size) if j == 0 else pl.ds(ROWS + j * size, width * size)

    def copy(way, column, level, j, width):
        slot = slot_of(column, level, core)
        part = tiles_ref.at[slot, rows_of(j, width)]
        return pltpu.make_async_remote_copy(
            src_ref=part, dst_ref=part, send_sem=send_sem.at[way, level * DEPTH + COLUMNS.index(column)],
            recv_sem=cross_sem.at[slot, j // 2] if way == C else recv_sem.at[slot, j],
            device_id=target[way], device_id_type=MESH,
        )

    def landed(slot, rows, sem):
        part = tiles_ref.at[slot, rows]
        pltpu.make_async_remote_copy(
            src_ref=part, dst_ref=part, send_sem=send_sem.at[0, 0], recv_sem=sem,
            device_id=target[C], device_id_type=MESH,
        ).wait_recv()

    def left(way, column, level, panels):
        part = tiles_ref.at[slot_of(column, level, core), pl.ds(0, len(panels) * size + (ROWS if 0 in panels else 0))]
        pltpu.make_async_remote_copy(
            src_ref=part, dst_ref=part, send_sem=send_sem.at[way, level * DEPTH + COLUMNS.index(column)],
            recv_sem=recv_sem.at[0, 0], device_id=target[way], device_id_type=MESH,
        ).wait_send()

    ops, _ = play_orders()
    groups = {}
    for end in (True, False):
        groups[end] = [[]]
        for op in ops[end]:
            if op[0] == "work":
                groups[end].append([])
            else:
                groups[end][-1].append(op)

    def play(end, index):
        for name, way, (column, level, j) in groups[end][index]:
            if name == "take":
                slot = slot_of(column, level, core)
                landed(slot, rows_of(j), recv_sem.at[slot, j])
            elif name == "across":
                slot = slot_of(column, level, 1 - core)
                landed(slot, rows_of(2 * j, 2), cross_sem.at[slot, j])
            elif name == "start":
                copy(way, column, level, j, 1).start()
            elif name == "cross":
                copy(C, column, level, 2 * j, 2).start()
            else:
                left(way, column, level, j)

    def both_kinds(act):
        pl.when(at_end)(lambda: act(True))
        pl.when(inner)(lambda: act(False))

    halves = EACH // 2

    both_kinds(lambda end: play(end, 0))

    wanted_row = jnp.full((ROWS, LANES), -2, jnp.int32)
    wanted_col = wanted_row
    for b in range(blocks):
        wanted_row = jnp.where(lane == b, rows_in[z * blocks + b], wanted_row)
        wanted_col = jnp.where(lane == b, cols_in[z * blocks + b], wanted_col)
    table_ref[0] = wanted_row
    table_ref[1] = wanted_col

    def clear_total(b, _):
        total_ref[b] = jnp.zeros((size, size), jnp.float32)
        return 0

    lax.fori_loop(0, blocks, clear_total, 0)
    made_ref[KEPT] = jnp.zeros((size, size), jnp.float32)
    before = (
        lax.broadcasted_iota(jnp.int32, (LANES, LANES), 0) < lax.broadcasted_iota(jnp.int32, (LANES, LANES), 1)
    ).astype(jnp.float32)

    table_copy = pltpu.make_async_copy(table_ref.at[pl.ds(2, 2)], index_ref, table_sem)

    def make_table(level):
        want_row, want_col = table_ref[0].astype(jnp.float32), table_ref[1].astype(jnp.float32)
        slot_row = jnp.full((ROWS, LANES), -1, jnp.int32)
        slot_col = slot_row
        for t in range(terms):
            listed = tiles_ref[level * terms + t, :ROWS]
            slot_row = jnp.where(listed == want_row, t, slot_row)
            slot_col = jnp.where(listed == want_col, t, slot_col)
        present = (slot_row >= 0) & (slot_col >= 0)
        code = ((lane * 2 + sub % 2) * terms + slot_row) * terms + slot_col
        ones = jnp.where(present, 1.0, 0.0).astype(jnp.float32)
        ahead = jnp.dot(ones, before, preferred_element_type=jnp.float32)
        count = jnp.sum(ones, axis=1, keepdims=True)
        twin = jnp.concatenate([count[:1] * 0.0, count[: ROWS - 1]], axis=0)
        ahead = ahead + jnp.where(sub % 2 == 1, twin, 0.0)
        place = jnp.clip(jnp.where(present, ahead, float(LANES)).astype(jnp.int32), 0, LANES)
        table_ref[3] = jnp.minimum(place, KEPT)
        entries = jnp.where(lane == LANES - 1, count.astype(jnp.int32), 0)
        for b in range(blocks):
            entries = entries + jnp.where(place[:, b : b + 1] == lane, code[:, b : b + 1], 0)
        table_ref[2] = entries
        for half in range(halves):
            both = entries[2 * half : 2 * half + 1] + entries[2 * half + 1 : 2 * half + 2]
            table_ref[2, half : half + 1] = both
            list_ref[pl.ds(level * halves + half, 1)] = both
        table_copy.start()

    def products(half, first):
        picked = [index_ref[0, half, first + k] for k in range(BATCH)]
        values = []
        for code in picked:
            pair = code % (2 * terms * terms)
            left = (pair // (terms * terms)) * terms + (pair // terms) % terms
            right = (pair // (terms * terms)) * terms + pair % terms
            values.append(jnp.dot(left_ref[left], right_ref[right], preferred_element_type=jnp.float32))
        for k, value in enumerate(values):
            made_ref[first + k] = value

    def collect(half):
        def one(b, _):
            j = half * 2
            total_ref[b] = total_ref[b] + (made_ref[index_ref[1, j, b]] + made_ref[index_ref[1, j + 1, b]])
            return 0

        lax.fori_loop(0, blocks, one, 0, unroll=8)

    def transfers(k, step):
        for at in range(PAIRS - 1):
            pl.when(k == at)(lambda: both_kinds(lambda end: play(end, at * 4 + step + 1)))

    def pair(k, _):
        half = k % halves
        near = k // halves
        level = level_of(jnp.where(at_end | (near >= 2), near, 1 - near))
        transfers(k, 0)
        pl.when(half == 0)(lambda: make_table(level))
        for j in range(2):
            row = pl.multiple_of(ROWS + (half * 2 + j) * size, ROWS)
            for t in range(terms):
                prepare(tiles_ref[level * terms + t, pl.ds(row, size)], j * terms + t, left_ref, right_ref)
        pl.when(half == 0)(lambda: table_copy.wait())
        transfers(k, 1)
        products(half, 0)
        transfers(k, 2)
        products(half, BATCH)
        transfers(k, 3)
        collect(half)
        return 0

    lax.fori_loop(0, PAIRS - 1, pair, 0)
    both_kinds(lambda end: play(end, PAIRS * 4 - 3))


def gather_by_hand(ids, rows, cols, shard, blocks):
    terms = CORES * SIDE * SIDE
    size = shard.shape[1]
    vmem = pl.BlockSpec(memory_space=pltpu.VMEM)
    return pl.pallas_call(
        functools.partial(gather_kernel, blocks),
        out_shape=(
            pltpu.VMEM((DEPTH * terms, ROWS + shard.shape[0], size), jnp.float32),
            pltpu.VMEM((blocks + 1, size, size), jnp.float32),
            pltpu.VMEM((ROWS, LANES), jnp.int32),
        ),
        in_specs=[pl.BlockSpec(memory_space=pltpu.HBM)] * 4,
        out_specs=(vmem, vmem, vmem),
        scratch_shapes=[
            pltpu.SMEM(ids.shape, jnp.int32),
            pltpu.SMEM(rows.shape, jnp.int32),
            pltpu.SMEM(cols.shape, jnp.int32),
            pltpu.VMEM((KEPT + 1, size, size), jnp.float32),
            pltpu.VMEM((2 * terms, size, 3 * size), jnp.bfloat16),
            pltpu.VMEM((2 * terms, 3 * size, size), jnp.bfloat16),
            pltpu.VMEM((4, ROWS, LANES), jnp.int32),
            pltpu.SMEM((2, ROWS, LANES), jnp.int32),
            pltpu.SemaphoreType.DMA((3,)),
            pltpu.SemaphoreType.DMA,
            pltpu.SemaphoreType.DMA,
            pltpu.SemaphoreType.DMA((5, DEPTH * len(COLUMNS))),
            pltpu.SemaphoreType.DMA((DEPTH * terms, EACH)),
            pltpu.SemaphoreType.DMA((DEPTH * terms, EACH // 2)),
        ],
        compiler_params=pltpu.CompilerParams(
            collective_id=0, has_side_effects=True, vmem_limit_bytes=30 * 1024 * 1024
        ),
    )(*(pltpu.with_memory_space_constraint(value, pltpu.HBM) for value in (ids, rows, cols, shard)))


def split(value):
    high = value.astype(jnp.bfloat16)
    return high, (value - high.astype(jnp.float32)).astype(jnp.bfloat16)


def prepare(value, s, left_ref, right_ref):
    size = value.shape[0]
    high, low = split(value)
    right_ref[s, :size] = high
    right_ref[s, size : 2 * size] = high
    right_ref[s, 2 * size :] = low
    high, low = split(value.T)
    left_ref[s, :, :size] = high
    left_ref[s, :, size : 2 * size] = low
    left_ref[s, :, 2 * size :] = high


def add_products(slots, read, count, out_ref, left_ref, right_ref, filled):
    def entries(first, width):
        picked = []
        for k in range(width):
            code = read(first + k)
            pair = code % (slots * slots)
            picked.append((code // (slots * slots), pair // slots, pair % slots))
        sums = [
            out_ref[b] + jnp.dot(left_ref[r], right_ref[c], preferred_element_type=jnp.float32)
            for b, r, c in picked
        ]
        for (b, _, _), value in zip(picked, sums):
            out_ref[b] = value

    groups = (count + UNROLL - 1) // UNROLL if filled else count // UNROLL
    pl.loop(0, groups)(lambda i: entries(i * UNROLL, UNROLL))
    if filled:
        return
    pl.loop(groups * UNROLL, count)(lambda i: entries(i, 1))


def clear(out_ref):
    def one(b, _):
        out_ref[b] = jnp.zeros(out_ref.shape[1:], jnp.float32)
        return 0

    lax.fori_loop(0, out_ref.shape[0], one, 0)


def held_kernel(blocks, tiles_ref, total_in, list_in, out_ref, total_ref, left_ref, right_ref, list_ref, list_sem, out_sem):
    terms = CORES * SIDE * SIDE
    size = tiles_ref.shape[2]
    z = lax.axis_index("rep")
    fetch = pltpu.make_async_copy(list_in, list_ref, list_sem)
    fetch.start()

    def get_ready(place):
        slot = place // 2 * terms
        for j in range(2):
            row = pl.multiple_of(ROWS + (place % 2 * 2 + j) * size, ROWS)
            for s in range(terms):
                prepare(tiles_ref[slot + s, pl.ds(row, size)], j * terms + s, left_ref, right_ref)

    def add(place, first, width):
        values = []
        for k in range(width):
            code = list_ref[place, first + k]
            pair = code % (2 * terms * terms)
            left = (pair // (terms * terms)) * terms + (pair // terms) % terms
            right = (pair // (terms * terms)) * terms + pair % terms
            value = jnp.dot(left_ref[left], right_ref[right], preferred_element_type=jnp.float32)
            values.append((jnp.where(first + k < list_ref[place, LANES - 1], code // (2 * terms * terms), blocks), value))
        for b, value in values:
            total_ref[b] = total_ref[b] + value

    def add_from(place, first):
        groups = (list_ref[place, LANES - 1] - first + LATE_BATCH - 1) // LATE_BATCH
        pl.loop(0, groups)(lambda i: add(place, first + i * LATE_BATCH, LATE_BATCH))

    last = jnp.where(z >= DEPTH // 2, 1, PAIRS - 1)
    get_ready(last)
    fetch.wait()
    add_from(last, 0)

    def rest(place):
        def more():
            get_ready(place)
            add_from(place, KEPT)

        pl.when((place != last) & (list_ref[place, LANES - 1] > KEPT))(more)

    pl.loop(0, PAIRS)(rest)
    pieces = out_sem.shape[0]
    each = blocks // pieces
    outs = [
        pltpu.make_async_copy(total_ref.at[pl.ds(i * each, each)], out_ref.at[pl.ds(i * each, each)], out_sem.at[i])
        for i in range(pieces)
    ]
    for out in outs:
        out.start()
    for out in outs:
        out.wait()


def held_products(tiles, total, entries, blocks):
    size = tiles.shape[2]
    terms = CORES * SIDE * SIDE
    pieces = next(n for n in (8, 7, 4, 2, 1) if blocks % n == 0)
    vmem = pl.BlockSpec(memory_space=pltpu.VMEM)
    return pl.pallas_call(
        functools.partial(held_kernel, blocks),
        out_shape=(
            jax.ShapeDtypeStruct((blocks, size, size), jnp.float32),
            pltpu.VMEM(total.shape, jnp.float32),
        ),
        in_specs=[vmem, vmem, vmem],
        out_specs=(pl.BlockSpec(memory_space=pl.ANY), vmem),
        input_output_aliases={1: 1},
        scratch_shapes=[
            pltpu.VMEM((2 * terms, size, 3 * size), jnp.bfloat16),
            pltpu.VMEM((2 * terms, 3 * size, size), jnp.bfloat16),
            pltpu.SMEM((ROWS, LANES), jnp.int32),
            pltpu.SemaphoreType.DMA,
            pltpu.SemaphoreType.DMA((pieces,)),
        ],
        compiler_params=pltpu.CompilerParams(vmem_limit_bytes=16 * 1024 * 1024),
    )(tiles, total, entries)[0]


def product_kernel(slots, base, count_ref, list_ref, tiles_ref, out_ref, left_ref, right_ref):
    panel = pl.program_id(0)

    pl.when(panel == 0)(lambda: clear(out_ref))
    pl.loop(0, slots)(lambda s: prepare(tiles_ref[0, s], s, left_ref, right_ref))
    add_products(
        slots, lambda k: list_ref[panel * base + k], count_ref[panel], out_ref, left_ref, right_ref, False
    )


def products(tiles, slots, panels_each, counts, entries, blocks):
    groups, size = tiles.shape[0], tiles.shape[3]
    return pl.pallas_call(
        functools.partial(product_kernel, slots, entries.shape[1]),
        out_shape=jax.ShapeDtypeStruct((blocks, size, size), jnp.float32),
        grid_spec=pltpu.PrefetchScalarGridSpec(
            num_scalar_prefetch=2,
            grid=(groups * panels_each,),
            in_specs=[
                pl.BlockSpec(
                    (1, slots, size, size), lambda p, *_: (p // panels_each, 0, p % panels_each, 0)
                )
            ],
            out_specs=pl.BlockSpec((blocks, size, size), lambda p, *_: (0, 0, 0)),
            scratch_shapes=[
                pltpu.VMEM((slots, size, 3 * size), jnp.bfloat16),
                pltpu.VMEM((slots, 3 * size, size), jnp.bfloat16),
            ],
        ),
        compiler_params=pltpu.CompilerParams(
            dimension_semantics=("arbitrary",), vmem_limit_bytes=56 * 1024 * 1024
        ),
    )(counts, entries.reshape(-1), tiles)


def block_list(ids, rows, cols):
    slots, blocks = ids.shape[1], rows.shape[0]
    order = jnp.arange(slots, dtype=jnp.int32)[None, :, None]
    match_row = ids[:, :, None] == rows[None, None, :]
    match_col = ids[:, :, None] == cols[None, None, :]
    slot_row = jnp.sum(jnp.where(match_row, order, 0), axis=1)
    slot_col = jnp.sum(jnp.where(match_col, order, 0), axis=1)
    present = jnp.any(match_row, axis=1) & jnp.any(match_col, axis=1)
    number = jnp.arange(blocks, dtype=jnp.int32)
    code = (number[None, :] * slots + slot_row) * slots + slot_col
    ahead = jnp.sum(
        jnp.where(present[:, None, :] & (number[None, None, :] < number[None, :, None]), 1, 0), axis=2
    )
    chosen = present[:, None, :] & (ahead[:, None, :] == number[None, :, None])
    entries = jnp.sum(jnp.where(chosen, code[:, None, :], 0), axis=2)
    counts = jnp.sum(present.astype(jnp.int32), axis=1)
    return counts.astype(jnp.int32), entries.astype(jnp.int32)


def solution(mesh):
    depth, terms = mesh.shape["rep"], mesh.shape["term"]

    def by_hand(panel_values, panel_ids, rows, cols, blocks):
        panels_each, _, passages, size = panel_values.shape
        tiles, total, entries = gather_by_hand(
            panel_ids.reshape(panels_each), rows, cols, panel_values.reshape(panels_each * passages, size), blocks
        )
        return held_products(tiles, total, entries, blocks)

    def local(panel_values, panel_ids, block_rows, block_cols):
        panels_each, own_slots, passages, size = panel_values.shape
        blocks = block_rows.shape[0] // depth
        slots = terms * own_slots
        shaped = own_slots == 1 and panels_each == EACH and passages == size == LANES
        if terms == CORES * SIDE * SIDE and depth == DEPTH and shaped and 2 * blocks + LATE_BATCH < LANES and blocks % 8 == 0:
            return by_hand(panel_values, panel_ids, block_rows, block_cols, blocks)
        first = lax.axis_index("rep") * blocks
        rows = lax.dynamic_slice_in_dim(block_rows, first, blocks)
        cols = lax.dynamic_slice_in_dim(block_cols, first, blocks)
        shard = jnp.swapaxes(panel_values, 0, 1).reshape(own_slots, panels_each * passages, size)
        tiles = lax.all_gather(shard, ("rep", "term"), axis=0, tiled=True)
        tiles = tiles.reshape(depth, slots, panels_each * passages, size)
        ids = lax.all_gather(panel_ids.T, ("rep", "term"), axis=0, tiled=True)
        ids = ids.reshape(depth, slots, panels_each)
        ids = jnp.swapaxes(ids, 1, 2).reshape(depth * panels_each, slots)
        counts, entries = block_list(ids, rows, cols)
        return products(tiles, slots, panels_each, counts, entries, blocks)

    placed = (P("rep", "term", None, None), P("rep", "term"), P("term"), P("term"))
    return jax.shard_map(
        local, mesh=mesh, in_specs=placed, out_specs=P(("term", "rep"), None, None), check_vma=False
    )
```

```python
import functools

import jax
import jax.numpy as jnp
from jax import lax
from jax.experimental import pallas as pl
from jax.experimental.pallas import tpu as pltpu
from jax.sharding import PartitionSpec as P

MESH = pl.DeviceIdType.MESH
CORES = 2
SIDE = 2
ROWS = 8
LANES = 128
DEPTH = 4
EACH = 4
UNROLL = 6
WINDOW = 2
LEVELS = {True: (0, 1, 2, 3), False: (1, 0, 2, 3)}
PAIRS = DEPTH * EACH // 2
KEPT = 28
WORKS = 4
BATCH = 14
LATE_BATCH = 10
T_LINK, T_HOP, T_CROSS, T_OP = 1.46, 2.2, 1.1, 0.08
T_SETUP, T_PREPARE, T_PRODUCTS, T_COLLECT = 1.0, 0.7, 0.5, 0.6
X, Y, C, IN, OUT = range(5)
FLIP_X = {"S": "X", "X": "S", "Y": "D", "D": "Y"}
FLIP_Y = {"S": "Y", "Y": "S", "X": "D", "D": "X"}
COLUMNS = ("S", "X", "Y", "D")


def link_orders(end):
    own, every = (0, range(EACH)) if end else (1, range(EACH))
    whole = lambda column, level: [(column, level, j) for j in every]

    def crossing(levels, rest, odd, other):
        order = []
        for level in levels:
            order += [(other, level, odd), (other, level, 2 + odd)]
            order += [("S", level, j + 1 - odd - 2 * (j % 2) * (1 - odd)) for j in every]
        for level in rest:
            order += whole("S", level)
        return order

    if end:
        return {
            X: crossing((0, 1), (2, 3), 0, "Y"),
            Y: crossing((0, 1), (2, 3), 1, "X"),
            IN: whole("S", 0) + whole("D", 0),
        }
    return {
        X: crossing((1,), (0, 2, 3), 0, "Y"),
        Y: crossing((1,), (0, 2, 3), 1, "X"),
        IN: whole("S", 1) + whole("D", 1) + whole("S", 0) + whole("D", 0),
        OUT: whole("S", 1) + whole("S", 2) + whole("D", 2) + whole("S", 3) + whole("D", 3),
    }


RECEIVERS = {
    (True, X): (True, lambda c: (FLIP_X[c[0]], c[1], c[2])),
    (True, Y): (True, lambda c: (FLIP_Y[c[0]], c[1], c[2])),
    (True, IN): (False, lambda c: c),
    (False, X): (False, lambda c: (FLIP_X[c[0]], c[1], c[2])),
    (False, Y): (False, lambda c: (FLIP_Y[c[0]], c[1], c[2])),
    (False, IN): (False, lambda c: (c[0], DEPTH - 1 - c[1], c[2])),
    (False, OUT): (True, lambda c: c),
}


def final_items(end):
    passed = {chunk[:2] for order in link_orders(end).values() for chunk in order}
    return {(column, level) for column in COLUMNS for level in range(DEPTH)} - passed


def play_orders():
    orders = {end: link_orders(end) for end in (True, False)}
    into = RECEIVERS
    works = {}
    for end in (True, False):
        pairs = [(level, half) for level in LEVELS[end] for half in range(EACH // 2)][: PAIRS - 1]
        works[end] = [(T_SETUP, [])]
        for level, half in pairs:
            needed = [(column, level, half) for column in COLUMNS]
            works[end] += [(T_PREPARE, needed), (T_PRODUCTS, []), (T_PRODUCTS, []), (T_COLLECT, [])]
    final = {end: final_items(end) for end in (True, False)}
    clock = {True: 0.0, False: 0.0}
    have = {end: {("S", 0 if end else 1, j) for j in range(EACH)} for end in (True, False)}
    coming = {True: [], False: []}
    across = {True: {}, False: {}}
    crossed = {True: set(), False: set()}
    flight = {key: [] for key in into}
    sent = {key: set() for key in into}
    free = {key: 0.0 for key in into}
    worked = {True: 0, False: 0}
    ops = {True: [], False: []}

    def cross(end, column, level, half):
        ops[end].append(("cross", None, (column, level, half)))
        across[end][column, level, half] = clock[end] + T_CROSS

    def act(end):
        now = clock[end]
        for arrival in sorted(coming[end]):
            if arrival[0] <= now:
                column, level, j = arrival[1]
                coming[end].remove(arrival)
                if (column, level) in final[end] and (column, level, j ^ 1) not in have[end]:
                    have[end].add(arrival[1])
                    return 0.0
                have[end].add(arrival[1])
                ops[end].append(("take", None, arrival[1]))
                if (column, level, j ^ 1) in have[end]:
                    cross(end, column, level, j // 2)
                return T_OP
        for way, order in orders[end].items():
            key = (end, way)
            while flight[key] and flight[key][0] <= now:
                flight[key].pop(0)
            ready = [chunk for chunk in order if chunk in have[end] and chunk not in sent[key]]
            if ready and len(flight[key]) < WINDOW:
                chunk = ready[0]
                ops[end].append(("start", way, chunk))
                sent[key].add(chunk)
                free[key] = max(free[key], now) + T_LINK
                flight[key].append(free[key])
                receiver, rename = into[key]
                coming[receiver].append((free[key] + T_HOP, rename(chunk)))
                return T_OP
        if worked[end] < len(works[end]):
            lasts, needed = works[end][worked[end]]
            if all(across[end].get(c, now + 1) <= now for c in needed):
                ops[end] += [("across", None, c) for c in needed]
                crossed[end].update(needed)
                ops[end].append(("work", None, None))
                worked[end] += 1
                return lasts
        return None

    for end in (True, False):
        for half in range(EACH // 2):
            cross(end, "S", 0 if end else 1, half)
    while True:
        end = clock[True] <= clock[False]
        spent = act(end)
        if spent is not None:
            clock[end] += spent
            continue
        later = [t for t, _ in coming[end]] + list(across[end].values())
        later += [held[0] for (kind, _), held in flight.items() if kind == end and held]
        later = [t for t in later if t > clock[end]]
        other = clock[not end]
        if not later and act(not end) is None and not [t for t, _ in coming[not end] if t > other]:
            break
        clock[end] = min(later + [max(other, clock[end]) + T_OP])
    for end in (True, False):
        every = [(column, level, half) for column in COLUMNS for level in range(DEPTH) for half in range(EACH // 2)]
        ops[end] += [("across", None, c) for c in every if c not in crossed[end]]
        for way, order in orders[end].items():
            items = dict.fromkeys((chunk[0], chunk[1]) for chunk in order)
            for whole in (True, False):
                number = sum((column == "S" or way in (IN, OUT)) == whole for column, _ in items)
                if number:
                    ops[end].append(("settle", way, (number, whole, 0 if whole or way == X else 1)))
        ops[end].append(("settle", C, (len(COLUMNS) * DEPTH, True, 0)))
    return ops, clock


def gather_kernel(
    blocks, ids_hbm, rows_hbm, cols_hbm, shard_ref, tiles_ref, total_ref, list_ref, ids_in, rows_in, cols_in,
    made_ref, left_ref, right_ref, table_ref, index_ref,
    small_sem, own_sem, table_sem, send_sem, recv_sem, cross_sem,
):
    term = lax.axis_index("term")
    z = lax.axis_index("rep")
    core = term % CORES
    x = (term // CORES) % SIDE
    y = term // (CORES * SIDE)
    terms = CORES * SIDE * SIDE
    upper = (z >= DEPTH // 2).astype(jnp.int32)
    at_end = (z == 0) | (z == DEPTH - 1)
    inner = jnp.logical_not(at_end)
    inward = 1 - 2 * upper
    size = shard_ref.shape[1]

    def term_of(column, at_core):
        at_x = 1 - x if column in ("X", "D") else x
        at_y = 1 - y if column in ("Y", "D") else y
        return (at_y * SIDE + at_x) * CORES + at_core

    def level_of(level):
        return level + upper * (DEPTH - 1 - 2 * level)

    def slot_of(column, level, at_core):
        return level_of(level) * terms + term_of(column, at_core)

    target = {
        X: (term_of("X", core), z),
        Y: (term_of("Y", core), z),
        C: (term_of("S", 1 - core), z),
        IN: (term, z + inward),
        OUT: (term, z - inward),
    }
    smalls = [
        pltpu.make_async_copy(source, held, small_sem.at[i])
        for i, (source, held) in enumerate(((ids_hbm, ids_in), (rows_hbm, rows_in), (cols_hbm, cols_in)))
    ]
    for small in smalls:
        small.start()
    barrier = pltpu.get_barrier_semaphore()

    def greet(way):
        pl.semaphore_signal(barrier, inc=1, device_id=target[way], device_id_type=MESH)

    for way in (X, Y, C, IN):
        greet(way)
    pl.when(inner)(lambda: greet(OUT))
    own_slot = z * terms + term
    own = pltpu.make_async_copy(shard_ref, tiles_ref.at[own_slot, pl.ds(ROWS, EACH * size)], own_sem)
    own.start()
    sub = lax.broadcasted_iota(jnp.int32, (ROWS, LANES), 0)
    lane = lax.broadcasted_iota(jnp.int32, (ROWS, LANES), 1)
    ids = jnp.full((ROWS, LANES), -1, jnp.int32)
    for small in smalls:
        small.wait()
    for j in range(EACH):
        ids = jnp.where(sub == j, ids_in[j], ids)
    tiles_ref[own_slot, :ROWS] = ids.astype(jnp.float32)
    own.wait()
    pl.semaphore_wait(barrier, 4 + inner.astype(jnp.int32))

    def rows_of(j, width=1):
        return pl.ds(0, ROWS + width * size) if j == 0 else pl.ds(ROWS + j * size, width * size)

    final = {end: final_items(end) for end in (True, False)}

    def copy(end, way, column, level, j, width):
        mark = j
        if way != C:
            receiver, rename = RECEIVERS[end, way]
            if rename((column, level, j))[:2] in final[receiver]:
                mark = j & 2
        slot = slot_of(column, level, core)
        part = tiles_ref.at[slot, rows_of(j, width)]
        return pltpu.make_async_remote_copy(
            src_ref=part, dst_ref=part, send_sem=send_sem.at[way, int(way in (X, Y) and column != "S")],
            recv_sem=cross_sem.at[slot, j // 2] if way == C else recv_sem.at[slot, mark],
            device_id=target[way], device_id_type=MESH,
        )

    def landed(slot, rows, sem):
        part = tiles_ref.at[slot, rows]
        pltpu.make_async_remote_copy(
            src_ref=part, dst_ref=part, send_sem=send_sem.at[0, 0], recv_sem=sem,
            device_id=target[C], device_id_type=MESH,
        ).wait_recv()

    def left(way, number, whole, odd):
        rows = (EACH if whole else 2) * size + (0 if odd else ROWS)
        part = tiles_ref.at[pl.ds(0, number), pl.ds(0, rows)]
        pltpu.make_async_remote_copy(
            src_ref=part, dst_ref=part, send_sem=send_sem.at[way, int(not whole)], recv_sem=recv_sem.at[0, 0],
            device_id=target[way], device_id_type=MESH,
        ).wait_send()

    ops, _ = play_orders()
    groups = {}
    for end in (True, False):
        groups[end] = [[]]
        for op in ops[end]:
            if op[0] == "work":
                groups[end].append([])
            else:
                groups[end][-1].append(op)

    def play(end, index):
        for name, way, (column, level, j) in groups[end][index]:
            if name == "take":
                slot = slot_of(column, level, core)
                if (column, level) in final[end]:
                    landed(slot, rows_of(j & 2, 2), recv_sem.at[slot, j & 2])
                else:
                    landed(slot, rows_of(j), recv_sem.at[slot, j])
            elif name == "across":
                slot = slot_of(column, level, 1 - core)
                landed(slot, rows_of(2 * j, 2), cross_sem.at[slot, j])
            elif name == "start":
                copy(end, way, column, level, j, 1).start()
            elif name == "cross":
                copy(end, C, column, level, 2 * j, 2).start()
            else:
                left(way, column, level, j)

    def both_kinds(act):
        lax.cond(at_end, lambda: act(True), lambda: act(False))

    halves = EACH // 2

    both_kinds(lambda end: play(end, 0))

    wanted_row = jnp.full((ROWS, LANES), -2, jnp.int32)
    wanted_col = wanted_row
    for b in range(blocks):
        wanted_row = jnp.where(lane == b, rows_in[z * blocks + b], wanted_row)
        wanted_col = jnp.where(lane == b, cols_in[z * blocks + b], wanted_col)
    table_ref[0] = wanted_row
    table_ref[1] = wanted_col

    def clear_total(b, _):
        total_ref[b] = jnp.zeros((size, size), jnp.float32)
        return 0

    lax.fori_loop(0, blocks, clear_total, 0)
    made_ref[KEPT] = jnp.zeros((size, size), jnp.float32)
    before = (
        lax.broadcasted_iota(jnp.int32, (LANES, LANES), 0) < lax.broadcasted_iota(jnp.int32, (LANES, LANES), 1)
    ).astype(jnp.float32)

    table_copy = pltpu.make_async_copy(table_ref.at[pl.ds(2, 2)], index_ref, table_sem)

    def make_table(level):
        want_row, want_col = table_ref[0].astype(jnp.float32), table_ref[1].astype(jnp.float32)
        slot_row = jnp.full((ROWS, LANES), -1, jnp.int32)
        slot_col = slot_row
        for t in range(terms):
            listed = tiles_ref[level * terms + t, :ROWS]
            slot_row = jnp.where(listed == want_row, t, slot_row)
            slot_col = jnp.where(listed == want_col, t, slot_col)
        present = (slot_row >= 0) & (slot_col >= 0)
        code = ((lane * 2 + sub % 2) * terms + slot_row) * terms + slot_col
        ones = jnp.where(present, 1.0, 0.0).astype(jnp.float32)
        ahead = jnp.dot(ones, before, preferred_element_type=jnp.float32)
        count = jnp.sum(ones, axis=1, keepdims=True)
        twin = jnp.concatenate([count[:1] * 0.0, count[: ROWS - 1]], axis=0)
        ahead = ahead + jnp.where(sub % 2 == 1, twin, 0.0)
        place = jnp.clip(jnp.where(present, ahead, float(LANES)).astype(jnp.int32), 0, LANES)
        table_ref[3] = jnp.minimum(place, KEPT)
        entries = jnp.where(lane == LANES - 1, count.astype(jnp.int32), 0)
        for b in range(blocks):
            entries = entries + jnp.where(place[:, b : b + 1] == lane, code[:, b : b + 1], 0)
        table_ref[2] = entries
        for half in range(halves):
            both = entries[2 * half : 2 * half + 1] + entries[2 * half + 1 : 2 * half + 2]
            table_ref[2, half : half + 1] = both
            list_ref[pl.ds(level * halves + half, 1)] = both
        table_copy.start()

    def products(half, first):
        picked = [index_ref[0, half, first + k] for k in range(BATCH)]
        values = []
        for code in picked:
            pair = code % (2 * terms * terms)
            left = (pair // (terms * terms)) * terms + (pair // terms) % terms
            right = (pair // (terms * terms)) * terms + pair % terms
            values.append(jnp.dot(left_ref[left], right_ref[right], preferred_element_type=jnp.float32))
        for k, value in enumerate(values):
            made_ref[first + k] = value

    def collect(half):
        def one(b, _):
            j = half * 2
            total_ref[b] = total_ref[b] + (made_ref[index_ref[1, j, b]] + made_ref[index_ref[1, j + 1, b]])
            return 0

        lax.fori_loop(0, blocks, one, 0, unroll=8)

    def transfers(k, step):
        def choose(first, end_of):
            if end_of - first == 1:
                both_kinds(lambda end: play(end, first * WORKS + step + 1))
                return
            middle = (first + end_of) // 2
            lax.cond(k < middle, lambda: choose(first, middle), lambda: choose(middle, end_of))

        choose(0, PAIRS - 1)

    def pair(k, _):
        half = k % halves
        near = k // halves
        level = level_of(jnp.where(at_end | (near >= 2), near, 1 - near))
        transfers(k, 0)
        pl.when(half == 0)(lambda: make_table(level))
        for j in range(2):
            row = pl.multiple_of(ROWS + (half * 2 + j) * size, ROWS)
            for t in range(terms):
                prepare(tiles_ref[level * terms + t, pl.ds(row, size)], j * terms + t, left_ref, right_ref)
        pl.when(half == 0)(lambda: table_copy.wait())
        transfers(k, 1)
        products(half, 0)
        transfers(k, 2)
        products(half, BATCH)
        transfers(k, 3)
        collect(half)
        return 0

    lax.fori_loop(0, PAIRS - 1, pair, 0)
    both_kinds(lambda end: play(end, (PAIRS - 1) * WORKS + 1))


def gather_by_hand(ids, rows, cols, shard, blocks):
    terms = CORES * SIDE * SIDE
    size = shard.shape[1]
    vmem = pl.BlockSpec(memory_space=pltpu.VMEM)
    return pl.pallas_call(
        functools.partial(gather_kernel, blocks),
        out_shape=(
            pltpu.VMEM((DEPTH * terms, ROWS + shard.shape[0], size), jnp.float32),
            pltpu.VMEM((blocks + 1, size, size), jnp.float32),
            pltpu.VMEM((ROWS, LANES), jnp.int32),
        ),
        in_specs=[pl.BlockSpec(memory_space=pltpu.HBM)] * 4,
        out_specs=(vmem, vmem, vmem),
        scratch_shapes=[
            pltpu.SMEM(ids.shape, jnp.int32),
            pltpu.SMEM(rows.shape, jnp.int32),
            pltpu.SMEM(cols.shape, jnp.int32),
            pltpu.VMEM((KEPT + 1, size, size), jnp.float32),
            pltpu.VMEM((2 * terms, size, 3 * size), jnp.bfloat16),
            pltpu.VMEM((2 * terms, 3 * size, size), jnp.bfloat16),
            pltpu.VMEM((4, ROWS, LANES), jnp.int32),
            pltpu.SMEM((2, ROWS, LANES), jnp.int32),
            pltpu.SemaphoreType.DMA((3,)),
            pltpu.SemaphoreType.DMA,
            pltpu.SemaphoreType.DMA,
            pltpu.SemaphoreType.DMA((5, 2)),
            pltpu.SemaphoreType.DMA((DEPTH * terms, EACH)),
            pltpu.SemaphoreType.DMA((DEPTH * terms, EACH // 2)),
        ],
        compiler_params=pltpu.CompilerParams(
            collective_id=0, has_side_effects=True, vmem_limit_bytes=30 * 1024 * 1024
        ),
    )(*(pltpu.with_memory_space_constraint(value, pltpu.HBM) for value in (ids, rows, cols, shard)))


def split(value):
    high = value.astype(jnp.bfloat16)
    return high, (value - high.astype(jnp.float32)).astype(jnp.bfloat16)


def prepare(value, s, left_ref, right_ref):
    size = value.shape[0]
    high, low = split(value)
    right_ref[s, :size] = high
    right_ref[s, size : 2 * size] = high
    right_ref[s, 2 * size :] = low
    high, low = split(value.T)
    left_ref[s, :, :size] = high
    left_ref[s, :, size : 2 * size] = low
    left_ref[s, :, 2 * size :] = high


def add_products(slots, read, count, out_ref, left_ref, right_ref, filled):
    def entries(first, width):
        picked = []
        for k in range(width):
            code = read(first + k)
            pair = code % (slots * slots)
            picked.append((code // (slots * slots), pair // slots, pair % slots))
        sums = [
            out_ref[b] + jnp.dot(left_ref[r], right_ref[c], preferred_element_type=jnp.float32)
            for b, r, c in picked
        ]
        for (b, _, _), value in zip(picked, sums):
            out_ref[b] = value

    groups = (count + UNROLL - 1) // UNROLL if filled else count // UNROLL
    pl.loop(0, groups)(lambda i: entries(i * UNROLL, UNROLL))
    if filled:
        return
    pl.loop(groups * UNROLL, count)(lambda i: entries(i, 1))


def clear(out_ref):
    def one(b, _):
        out_ref[b] = jnp.zeros(out_ref.shape[1:], jnp.float32)
        return 0

    lax.fori_loop(0, out_ref.shape[0], one, 0)


def held_kernel(blocks, tiles_ref, total_in, list_in, out_ref, total_ref, left_ref, right_ref, list_ref, list_sem, out_sem):
    terms = CORES * SIDE * SIDE
    size = tiles_ref.shape[2]
    z = lax.axis_index("rep")
    fetch = pltpu.make_async_copy(list_in, list_ref, list_sem)
    fetch.start()

    def get_ready(place):
        slot = place // 2 * terms
        for j in range(2):
            row = pl.multiple_of(ROWS + (place % 2 * 2 + j) * size, ROWS)
            for s in range(terms):
                prepare(tiles_ref[slot + s, pl.ds(row, size)], j * terms + s, left_ref, right_ref)

    def add(place, first, width):
        values = []
        for k in range(width):
            code = list_ref[place, first + k]
            pair = code % (2 * terms * terms)
            left = (pair // (terms * terms)) * terms + (pair // terms) % terms
            right = (pair // (terms * terms)) * terms + pair % terms
            value = jnp.dot(left_ref[left], right_ref[right], preferred_element_type=jnp.float32)
            values.append((jnp.where(first + k < list_ref[place, LANES - 1], code // (2 * terms * terms), blocks), value))
        for b, value in values:
            total_ref[b] = total_ref[b] + value

    def add_from(place, first):
        groups = (list_ref[place, LANES - 1] - first + LATE_BATCH - 1) // LATE_BATCH
        pl.loop(0, groups)(lambda i: add(place, first + i * LATE_BATCH, LATE_BATCH))

    last = jnp.where(z >= DEPTH // 2, 1, PAIRS - 1)
    get_ready(last)
    fetch.wait()
    add_from(last, 0)

    def rest(place):
        def more():
            get_ready(place)
            add_from(place, KEPT)

        pl.when((place != last) & (list_ref[place, LANES - 1] > KEPT))(more)

    pl.loop(0, PAIRS)(rest)
    pieces = out_sem.shape[0]
    each = blocks // pieces
    outs = [
        pltpu.make_async_copy(total_ref.at[pl.ds(i * each, each)], out_ref.at[pl.ds(i * each, each)], out_sem.at[i])
        for i in range(pieces)
    ]
    for out in outs:
        out.start()
    for out in outs:
        out.wait()


def held_products(tiles, total, entries, blocks):
    size = tiles.shape[2]
    terms = CORES * SIDE * SIDE
    pieces = next(n for n in (8, 7, 4, 2, 1) if blocks % n == 0)
    vmem = pl.BlockSpec(memory_space=pltpu.VMEM)
    return pl.pallas_call(
        functools.partial(held_kernel, blocks),
        out_shape=(
            jax.ShapeDtypeStruct((blocks, size, size), jnp.float32),
            pltpu.VMEM(total.shape, jnp.float32),
        ),
        in_specs=[vmem, vmem, vmem],
        out_specs=(pl.BlockSpec(memory_space=pl.ANY), vmem),
        input_output_aliases={1: 1},
        scratch_shapes=[
            pltpu.VMEM((2 * terms, size, 3 * size), jnp.bfloat16),
            pltpu.VMEM((2 * terms, 3 * size, size), jnp.bfloat16),
            pltpu.SMEM((ROWS, LANES), jnp.int32),
            pltpu.SemaphoreType.DMA,
            pltpu.SemaphoreType.DMA((pieces,)),
        ],
        compiler_params=pltpu.CompilerParams(vmem_limit_bytes=16 * 1024 * 1024),
    )(tiles, total, entries)[0]


def product_kernel(slots, base, count_ref, list_ref, tiles_ref, out_ref, left_ref, right_ref):
    panel = pl.program_id(0)

    pl.when(panel == 0)(lambda: clear(out_ref))
    pl.loop(0, slots)(lambda s: prepare(tiles_ref[0, s], s, left_ref, right_ref))
    add_products(
        slots, lambda k: list_ref[panel * base + k], count_ref[panel], out_ref, left_ref, right_ref, False
    )


def products(tiles, slots, panels_each, counts, entries, blocks):
    groups, size = tiles.shape[0], tiles.shape[3]
    return pl.pallas_call(
        functools.partial(product_kernel, slots, entries.shape[1]),
        out_shape=jax.ShapeDtypeStruct((blocks, size, size), jnp.float32),
        grid_spec=pltpu.PrefetchScalarGridSpec(
            num_scalar_prefetch=2,
            grid=(groups * panels_each,),
            in_specs=[
                pl.BlockSpec(
                    (1, slots, size, size), lambda p, *_: (p // panels_each, 0, p % panels_each, 0)
                )
            ],
            out_specs=pl.BlockSpec((blocks, size, size), lambda p, *_: (0, 0, 0)),
            scratch_shapes=[
                pltpu.VMEM((slots, size, 3 * size), jnp.bfloat16),
                pltpu.VMEM((slots, 3 * size, size), jnp.bfloat16),
            ],
        ),
        compiler_params=pltpu.CompilerParams(
            dimension_semantics=("arbitrary",), vmem_limit_bytes=56 * 1024 * 1024
        ),
    )(counts, entries.reshape(-1), tiles)


def block_list(ids, rows, cols):
    slots, blocks = ids.shape[1], rows.shape[0]
    order = jnp.arange(slots, dtype=jnp.int32)[None, :, None]
    match_row = ids[:, :, None] == rows[None, None, :]
    match_col = ids[:, :, None] == cols[None, None, :]
    slot_row = jnp.sum(jnp.where(match_row, order, 0), axis=1)
    slot_col = jnp.sum(jnp.where(match_col, order, 0), axis=1)
    present = jnp.any(match_row, axis=1) & jnp.any(match_col, axis=1)
    number = jnp.arange(blocks, dtype=jnp.int32)
    code = (number[None, :] * slots + slot_row) * slots + slot_col
    ahead = jnp.sum(
        jnp.where(present[:, None, :] & (number[None, None, :] < number[None, :, None]), 1, 0), axis=2
    )
    chosen = present[:, None, :] & (ahead[:, None, :] == number[None, :, None])
    entries = jnp.sum(jnp.where(chosen, code[:, None, :], 0), axis=2)
    counts = jnp.sum(present.astype(jnp.int32), axis=1)
    return counts.astype(jnp.int32), entries.astype(jnp.int32)


def solution(mesh):
    depth, terms = mesh.shape["rep"], mesh.shape["term"]

    def by_hand(panel_values, panel_ids, rows, cols, blocks):
        panels_each, _, passages, size = panel_values.shape
        tiles, total, entries = gather_by_hand(
            panel_ids.reshape(panels_each), rows, cols, panel_values.reshape(panels_each * passages, size), blocks
        )
        return held_products(tiles, total, entries, blocks)

    def local(panel_values, panel_ids, block_rows, block_cols):
        panels_each, own_slots, passages, size = panel_values.shape
        blocks = block_rows.shape[0] // depth
        slots = terms * own_slots
        shaped = own_slots == 1 and panels_each == EACH and passages == size == LANES
        if terms == CORES * SIDE * SIDE and depth == DEPTH and shaped and 2 * blocks + LATE_BATCH < LANES and blocks % 8 == 0:
            return by_hand(panel_values, panel_ids, block_rows, block_cols, blocks)
        first = lax.axis_index("rep") * blocks
        rows = lax.dynamic_slice_in_dim(block_rows, first, blocks)
        cols = lax.dynamic_slice_in_dim(block_cols, first, blocks)
        shard = jnp.swapaxes(panel_values, 0, 1).reshape(own_slots, panels_each * passages, size)
        tiles = lax.all_gather(shard, ("rep", "term"), axis=0, tiled=True)
        tiles = tiles.reshape(depth, slots, panels_each * passages, size)
        ids = lax.all_gather(panel_ids.T, ("rep", "term"), axis=0, tiled=True)
        ids = ids.reshape(depth, slots, panels_each)
        ids = jnp.swapaxes(ids, 1, 2).reshape(depth * panels_each, slots)
        counts, entries = block_list(ids, rows, cols)
        return products(tiles, slots, panels_each, counts, entries, blocks)

    placed = (P("rep", "term", None, None), P("rep", "term"), P("term"), P("term"))
    return jax.shard_map(
        local, mesh=mesh, in_specs=placed, out_specs=P(("term", "rep"), None, None), check_vma=False
    )
```

```python
import functools

import jax
import jax.numpy as jnp
from jax import lax
from jax.experimental import pallas as pl
from jax.experimental.pallas import tpu as pltpu
from jax.sharding import PartitionSpec as P

MESH = pl.DeviceIdType.MESH
CORES = 2
SIDE = 2
ROWS = 8
LANES = 128
DEPTH = 4
EACH = 4
UNROLL = 6
WINDOW = 2
LEVELS = {True: (0, 1, 2, 3), False: (1, 0, 2, 3)}
PAIRS = DEPTH * EACH // 2
KEPT = 28
WORKS = 4
BATCH = 14
LATE_BATCH = 14
T_LINK, T_HOP, T_CROSS, T_OP = 1.43, 2.3, 0.9, 0.075
T_SETUP, T_PREPARE, T_PRODUCTS, T_COLLECT = 1.0, 0.8, 0.55, 0.55
X, Y, C, IN, OUT = range(5)
FLIP_X = {"S": "X", "X": "S", "Y": "D", "D": "Y"}
FLIP_Y = {"S": "Y", "Y": "S", "X": "D", "D": "X"}
COLUMNS = ("S", "X", "Y", "D")


def link_orders(end):
    own, every = (0, range(EACH)) if end else (1, range(EACH))
    whole = lambda column, level: [(column, level, j) for j in every]

    def crossing(levels, rest, odd, other):
        order = []
        for level in levels:
            order += [(other, level, odd), (other, level, 2 + odd)]
            order += [("S", level, j + 1 - odd - 2 * (j % 2) * (1 - odd)) for j in every]
        for level in rest:
            order += whole("S", level)
        return order

    if end:
        return {
            X: crossing((0, 1), (2, 3), 0, "Y"),
            Y: crossing((0, 1), (2, 3), 1, "X"),
            IN: whole("S", 0) + whole("D", 0),
        }
    return {
        X: crossing((1,), (0, 2, 3), 0, "Y"),
        Y: crossing((1,), (0, 2, 3), 1, "X"),
        IN: whole("S", 1) + whole("D", 1) + whole("S", 0) + whole("D", 0),
        OUT: whole("S", 1) + whole("S", 2) + whole("D", 2) + whole("S", 3) + whole("D", 3),
    }


RECEIVERS = {
    (True, X): (True, lambda c: (FLIP_X[c[0]], c[1], c[2])),
    (True, Y): (True, lambda c: (FLIP_Y[c[0]], c[1], c[2])),
    (True, IN): (False, lambda c: c),
    (False, X): (False, lambda c: (FLIP_X[c[0]], c[1], c[2])),
    (False, Y): (False, lambda c: (FLIP_Y[c[0]], c[1], c[2])),
    (False, IN): (False, lambda c: (c[0], DEPTH - 1 - c[1], c[2])),
    (False, OUT): (True, lambda c: c),
}


def final_items(end):
    passed = {chunk[:2] for order in link_orders(end).values() for chunk in order}
    return {(column, level) for column in COLUMNS for level in range(DEPTH)} - passed


def play_orders():
    orders = {end: link_orders(end) for end in (True, False)}
    into = RECEIVERS
    works = {}
    for end in (True, False):
        pairs = [(level, half) for level in LEVELS[end] for half in range(EACH // 2)][: PAIRS - 1]
        works[end] = [(T_SETUP, [])]
        for level, half in pairs:
            needed = [(column, level, half) for column in COLUMNS]
            works[end] += [(T_PREPARE, needed), (T_PRODUCTS, []), (T_PRODUCTS, []), (T_COLLECT, [])]
    final = {end: final_items(end) for end in (True, False)}
    clock = {True: 0.0, False: 0.0}
    have = {end: {("S", 0 if end else 1, j) for j in range(EACH)} for end in (True, False)}
    coming = {True: [], False: []}
    across = {True: {}, False: {}}
    crossed = {True: set(), False: set()}
    flight = {key: [] for key in into}
    sent = {key: set() for key in into}
    free = {key: 0.0 for key in into}
    worked = {True: 0, False: 0}
    ops = {True: [], False: []}

    def cross(end, column, level, half):
        ops[end].append(("cross", None, (column, level, half)))
        across[end][column, level, half] = clock[end] + T_CROSS

    def act(end):
        now = clock[end]
        for arrival in sorted(coming[end]):
            if arrival[0] <= now:
                column, level, j = arrival[1]
                coming[end].remove(arrival)
                if (column, level) in final[end] and (column, level, j ^ 1) not in have[end]:
                    have[end].add(arrival[1])
                    return 0.0
                have[end].add(arrival[1])
                ops[end].append(("take", None, arrival[1]))
                if (column, level, j ^ 1) in have[end]:
                    cross(end, column, level, j // 2)
                return T_OP
        for way, order in orders[end].items():
            key = (end, way)
            while flight[key] and flight[key][0] <= now:
                flight[key].pop(0)
            ready = [chunk for chunk in order if chunk in have[end] and chunk not in sent[key]]
            if ready and len(flight[key]) < WINDOW:
                chunk = ready[0]
                ops[end].append(("start", way, chunk))
                sent[key].add(chunk)
                free[key] = max(free[key], now) + T_LINK
                flight[key].append(free[key])
                receiver, rename = into[key]
                coming[receiver].append((free[key] + T_HOP, rename(chunk)))
                return T_OP
        if worked[end] < len(works[end]):
            lasts, needed = works[end][worked[end]]
            if all(across[end].get(c, now + 1) <= now for c in needed):
                ops[end] += [("across", None, c) for c in needed]
                crossed[end].update(needed)
                ops[end].append(("work", None, None))
                worked[end] += 1
                return lasts
        return None

    for end in (True, False):
        for half in range(EACH // 2):
            cross(end, "S", 0 if end else 1, half)
    while True:
        end = clock[True] <= clock[False]
        spent = act(end)
        if spent is not None:
            clock[end] += spent
            continue
        later = [t for t, _ in coming[end]] + list(across[end].values())
        later += [held[0] for (kind, _), held in flight.items() if kind == end and held]
        later = [t for t in later if t > clock[end]]
        other = clock[not end]
        if not later and act(not end) is None and not [t for t, _ in coming[not end] if t > other]:
            break
        clock[end] = min(later + [max(other, clock[end]) + T_OP])
    for end in (True, False):
        every = [(column, level, half) for column in COLUMNS for level in range(DEPTH) for half in range(EACH // 2)]
        ops[end] += [("across", None, c) for c in every if c not in crossed[end]]
        for way, order in orders[end].items():
            items = dict.fromkeys((chunk[0], chunk[1]) for chunk in order)
            for whole in (True, False):
                number = sum((column == "S" or way in (IN, OUT)) == whole for column, _ in items)
                if number:
                    ops[end].append(("settle", way, (number, whole, 0 if whole or way == X else 1)))
        ops[end].append(("settle", C, (len(COLUMNS) * DEPTH, True, 0)))
    return ops, clock


def gather_kernel(
    blocks, ids_hbm, rows_hbm, cols_hbm, shard_ref, tiles_ref, total_ref, list_ref, ids_in, rows_in, cols_in,
    made_ref, left_ref, right_ref, table_ref, index_ref,
    small_sem, own_sem, table_sem, send_sem, recv_sem, cross_sem,
):
    term = lax.axis_index("term")
    z = lax.axis_index("rep")
    core = term % CORES
    x = (term // CORES) % SIDE
    y = term // (CORES * SIDE)
    terms = CORES * SIDE * SIDE
    upper = (z >= DEPTH // 2).astype(jnp.int32)
    at_end = (z == 0) | (z == DEPTH - 1)
    inner = jnp.logical_not(at_end)
    inward = 1 - 2 * upper
    size = shard_ref.shape[1]

    def term_of(column, at_core):
        at_x = 1 - x if column in ("X", "D") else x
        at_y = 1 - y if column in ("Y", "D") else y
        return (at_y * SIDE + at_x) * CORES + at_core

    def level_of(level):
        return level + upper * (DEPTH - 1 - 2 * level)

    def slot_of(column, level, at_core):
        return level_of(level) * terms + term_of(column, at_core)

    target = {
        X: (term_of("X", core), z),
        Y: (term_of("Y", core), z),
        C: (term_of("S", 1 - core), z),
        IN: (term, z + inward),
        OUT: (term, z - inward),
    }
    smalls = [
        pltpu.make_async_copy(source, held, small_sem.at[i])
        for i, (source, held) in enumerate(((ids_hbm, ids_in), (rows_hbm, rows_in), (cols_hbm, cols_in)))
    ]
    for small in smalls:
        small.start()
    barrier = pltpu.get_barrier_semaphore()

    def greet(way):
        pl.semaphore_signal(barrier, inc=1, device_id=target[way], device_id_type=MESH)

    for way in (X, Y, C, IN):
        greet(way)
    pl.when(inner)(lambda: greet(OUT))
    own_slot = z * terms + term
    own = pltpu.make_async_copy(shard_ref, tiles_ref.at[own_slot, pl.ds(ROWS, EACH * size)], own_sem)
    own.start()
    sub = lax.broadcasted_iota(jnp.int32, (ROWS, LANES), 0)
    lane = lax.broadcasted_iota(jnp.int32, (ROWS, LANES), 1)
    ids = jnp.full((ROWS, LANES), -1, jnp.int32)
    for small in smalls:
        small.wait()
    for j in range(EACH):
        ids = jnp.where(sub == j, ids_in[j], ids)
    tiles_ref[own_slot, :ROWS] = ids.astype(jnp.float32)
    own.wait()
    pl.semaphore_wait(barrier, 4 + inner.astype(jnp.int32))

    def rows_of(j, width=1):
        return pl.ds(0, ROWS + width * size) if j == 0 else pl.ds(ROWS + j * size, width * size)

    final = {end: final_items(end) for end in (True, False)}

    def copy(end, way, column, level, j, width):
        mark = j
        if way != C:
            receiver, rename = RECEIVERS[end, way]
            if rename((column, level, j))[:2] in final[receiver]:
                mark = j & 2
        slot = slot_of(column, level, core)
        part = tiles_ref.at[slot, rows_of(j, width)]
        return pltpu.make_async_remote_copy(
            src_ref=part, dst_ref=part, send_sem=send_sem.at[way, int(way in (X, Y) and column != "S")],
            recv_sem=cross_sem.at[slot, j // 2] if way == C else recv_sem.at[slot, mark],
            device_id=target[way], device_id_type=MESH,
        )

    def landed(slot, rows, sem):
        part = tiles_ref.at[slot, rows]
        pltpu.make_async_remote_copy(
            src_ref=part, dst_ref=part, send_sem=send_sem.at[0, 0], recv_sem=sem,
            device_id=target[C], device_id_type=MESH,
        ).wait_recv()

    def left(way, number, whole, odd):
        rows = (EACH if whole else 2) * size + (0 if odd else ROWS)
        part = tiles_ref.at[pl.ds(0, number), pl.ds(0, rows)]
        pltpu.make_async_remote_copy(
            src_ref=part, dst_ref=part, send_sem=send_sem.at[way, int(not whole)], recv_sem=recv_sem.at[0, 0],
            device_id=target[way], device_id_type=MESH,
        ).wait_send()

    ops, _ = play_orders()
    groups = {}
    for end in (True, False):
        groups[end] = [[]]
        for op in ops[end]:
            if op[0] == "work":
                groups[end].append([])
            else:
                groups[end][-1].append(op)

    def play(end, index):
        for name, way, (column, level, j) in groups[end][index]:
            if name == "take":
                slot = slot_of(column, level, core)
                if (column, level) in final[end]:
                    landed(slot, rows_of(j & 2, 2), recv_sem.at[slot, j & 2])
                else:
                    landed(slot, rows_of(j), recv_sem.at[slot, j])
            elif name == "across":
                slot = slot_of(column, level, 1 - core)
                landed(slot, rows_of(2 * j, 2), cross_sem.at[slot, j])
            elif name == "start":
                copy(end, way, column, level, j, 1).start()
            elif name == "cross":
                copy(end, C, column, level, 2 * j, 2).start()
            else:
                left(way, column, level, j)

    def both_kinds(act):
        lax.cond(at_end, lambda: act(True), lambda: act(False))

    halves = EACH // 2

    both_kinds(lambda end: play(end, 0))

    wanted_row = jnp.full((ROWS, LANES), -2, jnp.int32)
    wanted_col = wanted_row
    for b in range(blocks):
        wanted_row = jnp.where(lane == b, rows_in[z * blocks + b], wanted_row)
        wanted_col = jnp.where(lane == b, cols_in[z * blocks + b], wanted_col)
    table_ref[0] = wanted_row
    table_ref[1] = wanted_col

    def clear_total(b, _):
        total_ref[b] = jnp.zeros((size, size), jnp.float32)
        return 0

    lax.fori_loop(0, blocks, clear_total, 0)
    made_ref[KEPT] = jnp.zeros((size, size), jnp.float32)
    before = (
        lax.broadcasted_iota(jnp.int32, (LANES, LANES), 0) < lax.broadcasted_iota(jnp.int32, (LANES, LANES), 1)
    ).astype(jnp.float32)

    table_copy = pltpu.make_async_copy(table_ref.at[pl.ds(2, 2)], index_ref, table_sem)

    def make_table(level):
        want_row, want_col = table_ref[0].astype(jnp.float32), table_ref[1].astype(jnp.float32)
        slot_row = jnp.full((ROWS, LANES), -1, jnp.int32)
        slot_col = slot_row
        for t in range(terms):
            listed = tiles_ref[level * terms + t, :ROWS]
            slot_row = jnp.where(listed == want_row, t, slot_row)
            slot_col = jnp.where(listed == want_col, t, slot_col)
        present = (slot_row >= 0) & (slot_col >= 0)
        ones = jnp.where(present, 1.0, 0.0).astype(jnp.float32)
        ahead = jnp.dot(ones, before, preferred_element_type=jnp.float32)
        count = jnp.sum(ones, axis=1, keepdims=True)
        twin = jnp.concatenate([count[:1] * 0.0, count[: ROWS - 1]], axis=0)
        ahead = ahead + jnp.where(sub % 2 == 1, twin, 0.0)
        place = jnp.clip(jnp.where(present, ahead, float(LANES)).astype(jnp.int32), 0, LANES)
        table_ref[3] = jnp.minimum(place, KEPT)
        upper_part = jnp.where(present, lane * 2 + sub % 2, 0).astype(jnp.float32)
        lower_part = jnp.where(present, slot_row * terms + slot_col, 0).astype(jnp.float32)
        parts = [
            jnp.concatenate([jnp.where(sub == j, part, 0.0) for j in range(EACH)], axis=1)
            for part in (upper_part, lower_part)
        ]
        deep = lax.broadcasted_iota(jnp.int32, (LANES, LANES), 0)
        chosen = jnp.concatenate(
            [jnp.where(place[j : j + 1] == deep, 1.0, 0.0).astype(jnp.bfloat16) for j in range(EACH)], axis=1
        )
        found = lax.dot_general(
            jnp.concatenate(parts, axis=0).astype(jnp.bfloat16), chosen, (((1,), (1,)), ((), ())),
            preferred_element_type=jnp.float32,
        )
        codes = found[:ROWS] * float(terms * terms) + found[ROWS:]
        codes = jnp.clip(codes.astype(jnp.int32), 0, 2 * blocks * terms * terms)
        entries = jnp.where(lane == LANES - 1, count.astype(jnp.int32), codes)
        table_ref[2] = entries
        for half in range(halves):
            both = entries[2 * half : 2 * half + 1] + entries[2 * half + 1 : 2 * half + 2]
            table_ref[2, half : half + 1] = both
            list_ref[pl.ds(level * halves + half, 1)] = both
        table_copy.start()

    def products(half, first):
        picked = [index_ref[0, half, first + k] for k in range(BATCH)]
        values = []
        for code in picked:
            pair = code % (2 * terms * terms)
            left = (pair // (terms * terms)) * terms + (pair // terms) % terms
            right = (pair // (terms * terms)) * terms + pair % terms
            values.append(jnp.dot(left_ref[left], right_ref[right], preferred_element_type=jnp.float32))
        for k, value in enumerate(values):
            made_ref[first + k] = value

    def collect(half):
        def one(b, _):
            j = half * 2
            total_ref[b] = total_ref[b] + (made_ref[index_ref[1, j, b]] + made_ref[index_ref[1, j + 1, b]])
            return 0

        lax.fori_loop(0, blocks, one, 0, unroll=8)

    def transfers(k, step):
        def choose(first, end_of):
            if end_of - first == 1:
                both_kinds(lambda end: play(end, first * WORKS + step + 1))
                return
            middle = (first + end_of) // 2
            lax.cond(k < middle, lambda: choose(first, middle), lambda: choose(middle, end_of))

        choose(0, PAIRS - 1)

    def pair(k, _):
        half = k % halves
        near = k // halves
        level = level_of(jnp.where(at_end | (near >= 2), near, 1 - near))
        transfers(k, 0)
        pl.when(half == 0)(lambda: make_table(level))
        for j in range(2):
            row = pl.multiple_of(ROWS + (half * 2 + j) * size, ROWS)
            for t in range(terms):
                prepare(tiles_ref[level * terms + t, pl.ds(row, size)], j * terms + t, left_ref, right_ref)
        pl.when(half == 0)(lambda: table_copy.wait())
        transfers(k, 1)
        products(half, 0)
        transfers(k, 2)
        products(half, BATCH)
        transfers(k, 3)
        collect(half)
        return 0

    lax.fori_loop(0, PAIRS - 1, pair, 0)
    both_kinds(lambda end: play(end, (PAIRS - 1) * WORKS + 1))


def gather_by_hand(ids, rows, cols, shard, blocks):
    terms = CORES * SIDE * SIDE
    size = shard.shape[1]
    vmem = pl.BlockSpec(memory_space=pltpu.VMEM)
    return pl.pallas_call(
        functools.partial(gather_kernel, blocks),
        out_shape=(
            pltpu.VMEM((DEPTH * terms, ROWS + shard.shape[0], size), jnp.float32),
            pltpu.VMEM((blocks + 1, size, size), jnp.float32),
            pltpu.VMEM((ROWS, LANES), jnp.int32),
        ),
        in_specs=[pl.BlockSpec(memory_space=pltpu.HBM)] * 4,
        out_specs=(vmem, vmem, vmem),
        scratch_shapes=[
            pltpu.SMEM(ids.shape, jnp.int32),
            pltpu.SMEM(rows.shape, jnp.int32),
            pltpu.SMEM(cols.shape, jnp.int32),
            pltpu.VMEM((KEPT + 1, size, size), jnp.float32),
            pltpu.VMEM((2 * terms, size, 3 * size), jnp.bfloat16),
            pltpu.VMEM((2 * terms, 3 * size, size), jnp.bfloat16),
            pltpu.VMEM((4, ROWS, LANES), jnp.int32),
            pltpu.SMEM((2, ROWS, LANES), jnp.int32),
            pltpu.SemaphoreType.DMA((3,)),
            pltpu.SemaphoreType.DMA,
            pltpu.SemaphoreType.DMA,
            pltpu.SemaphoreType.DMA((5, 2)),
            pltpu.SemaphoreType.DMA((DEPTH * terms, EACH)),
            pltpu.SemaphoreType.DMA((DEPTH * terms, EACH // 2)),
        ],
        compiler_params=pltpu.CompilerParams(
            collective_id=0, has_side_effects=True, vmem_limit_bytes=30 * 1024 * 1024
        ),
    )(*(pltpu.with_memory_space_constraint(value, pltpu.HBM) for value in (ids, rows, cols, shard)))


def split(value):
    high = value.astype(jnp.bfloat16)
    return high, (value - high.astype(jnp.float32)).astype(jnp.bfloat16)


def prepare(value, s, left_ref, right_ref):
    size = value.shape[0]
    high, low = split(value)
    right_ref[s, :size] = high
    right_ref[s, size : 2 * size] = high
    right_ref[s, 2 * size :] = low
    high, low = split(value.T)
    left_ref[s, :, :size] = high
    left_ref[s, :, size : 2 * size] = low
    left_ref[s, :, 2 * size :] = high


def add_products(slots, read, count, out_ref, left_ref, right_ref, filled):
    def entries(first, width):
        picked = []
        for k in range(width):
            code = read(first + k)
            pair = code % (slots * slots)
            picked.append((code // (slots * slots), pair // slots, pair % slots))
        sums = [
            out_ref[b] + jnp.dot(left_ref[r], right_ref[c], preferred_element_type=jnp.float32)
            for b, r, c in picked
        ]
        for (b, _, _), value in zip(picked, sums):
            out_ref[b] = value

    groups = (count + UNROLL - 1) // UNROLL if filled else count // UNROLL
    pl.loop(0, groups)(lambda i: entries(i * UNROLL, UNROLL))
    if filled:
        return
    pl.loop(groups * UNROLL, count)(lambda i: entries(i, 1))


def clear(out_ref):
    def one(b, _):
        out_ref[b] = jnp.zeros(out_ref.shape[1:], jnp.float32)
        return 0

    lax.fori_loop(0, out_ref.shape[0], one, 0)


def held_kernel(blocks, tiles_ref, total_in, list_in, out_ref, total_ref, left_ref, right_ref, list_ref, list_sem, out_sem):
    terms = CORES * SIDE * SIDE
    size = tiles_ref.shape[2]
    z = lax.axis_index("rep")
    fetch = pltpu.make_async_copy(list_in, list_ref, list_sem)
    fetch.start()

    def get_ready(place):
        slot = place // 2 * terms
        for j in range(2):
            row = pl.multiple_of(ROWS + (place % 2 * 2 + j) * size, ROWS)
            for s in range(terms):
                prepare(tiles_ref[slot + s, pl.ds(row, size)], j * terms + s, left_ref, right_ref)

    def add(place, first, width):
        values = []
        for k in range(width):
            code = list_ref[place, first + k]
            pair = code % (2 * terms * terms)
            left = (pair // (terms * terms)) * terms + (pair // terms) % terms
            right = (pair // (terms * terms)) * terms + pair % terms
            value = jnp.dot(left_ref[left], right_ref[right], preferred_element_type=jnp.float32)
            values.append((jnp.where(first + k < list_ref[place, LANES - 1], code // (2 * terms * terms), blocks), value))
        for b, value in values:
            total_ref[b] = total_ref[b] + value

    def add_from(place, first):
        groups = (list_ref[place, LANES - 1] - first + LATE_BATCH - 1) // LATE_BATCH
        pl.loop(0, groups)(lambda i: add(place, first + i * LATE_BATCH, LATE_BATCH))

    last = jnp.where(z >= DEPTH // 2, 1, PAIRS - 1)
    get_ready(last)
    fetch.wait()
    add_from(last, 0)

    def rest(place):
        def more():
            get_ready(place)
            add_from(place, KEPT)

        pl.when((place != last) & (list_ref[place, LANES - 1] > KEPT))(more)

    pl.loop(0, PAIRS)(rest)
    pieces = out_sem.shape[0]
    each = blocks // pieces
    outs = [
        pltpu.make_async_copy(total_ref.at[pl.ds(i * each, each)], out_ref.at[pl.ds(i * each, each)], out_sem.at[i])
        for i in range(pieces)
    ]
    for out in outs:
        out.start()
    for out in outs:
        out.wait()


def held_products(tiles, total, entries, blocks):
    size = tiles.shape[2]
    terms = CORES * SIDE * SIDE
    pieces = next(n for n in (8, 7, 4, 2, 1) if blocks % n == 0)
    vmem = pl.BlockSpec(memory_space=pltpu.VMEM)
    return pl.pallas_call(
        functools.partial(held_kernel, blocks),
        out_shape=(
            jax.ShapeDtypeStruct((blocks, size, size), jnp.float32),
            pltpu.VMEM(total.shape, jnp.float32),
        ),
        in_specs=[vmem, vmem, vmem],
        out_specs=(pl.BlockSpec(memory_space=pl.ANY), vmem),
        input_output_aliases={1: 1},
        scratch_shapes=[
            pltpu.VMEM((2 * terms, size, 3 * size), jnp.bfloat16),
            pltpu.VMEM((2 * terms, 3 * size, size), jnp.bfloat16),
            pltpu.SMEM((ROWS, LANES), jnp.int32),
            pltpu.SemaphoreType.DMA,
            pltpu.SemaphoreType.DMA((pieces,)),
        ],
        compiler_params=pltpu.CompilerParams(vmem_limit_bytes=16 * 1024 * 1024),
    )(tiles, total, entries)[0]


def product_kernel(slots, base, count_ref, list_ref, tiles_ref, out_ref, left_ref, right_ref):
    panel = pl.program_id(0)

    pl.when(panel == 0)(lambda: clear(out_ref))
    pl.loop(0, slots)(lambda s: prepare(tiles_ref[0, s], s, left_ref, right_ref))
    add_products(
        slots, lambda k: list_ref[panel * base + k], count_ref[panel], out_ref, left_ref, right_ref, False
    )


def products(tiles, slots, panels_each, counts, entries, blocks):
    groups, size = tiles.shape[0], tiles.shape[3]
    return pl.pallas_call(
        functools.partial(product_kernel, slots, entries.shape[1]),
        out_shape=jax.ShapeDtypeStruct((blocks, size, size), jnp.float32),
        grid_spec=pltpu.PrefetchScalarGridSpec(
            num_scalar_prefetch=2,
            grid=(groups * panels_each,),
            in_specs=[
                pl.BlockSpec(
                    (1, slots, size, size), lambda p, *_: (p // panels_each, 0, p % panels_each, 0)
                )
            ],
            out_specs=pl.BlockSpec((blocks, size, size), lambda p, *_: (0, 0, 0)),
            scratch_shapes=[
                pltpu.VMEM((slots, size, 3 * size), jnp.bfloat16),
                pltpu.VMEM((slots, 3 * size, size), jnp.bfloat16),
            ],
        ),
        compiler_params=pltpu.CompilerParams(
            dimension_semantics=("arbitrary",), vmem_limit_bytes=56 * 1024 * 1024
        ),
    )(counts, entries.reshape(-1), tiles)


def block_list(ids, rows, cols):
    slots, blocks = ids.shape[1], rows.shape[0]
    order = jnp.arange(slots, dtype=jnp.int32)[None, :, None]
    match_row = ids[:, :, None] == rows[None, None, :]
    match_col = ids[:, :, None] == cols[None, None, :]
    slot_row = jnp.sum(jnp.where(match_row, order, 0), axis=1)
    slot_col = jnp.sum(jnp.where(match_col, order, 0), axis=1)
    present = jnp.any(match_row, axis=1) & jnp.any(match_col, axis=1)
    number = jnp.arange(blocks, dtype=jnp.int32)
    code = (number[None, :] * slots + slot_row) * slots + slot_col
    ahead = jnp.sum(
        jnp.where(present[:, None, :] & (number[None, None, :] < number[None, :, None]), 1, 0), axis=2
    )
    chosen = present[:, None, :] & (ahead[:, None, :] == number[None, :, None])
    entries = jnp.sum(jnp.where(chosen, code[:, None, :], 0), axis=2)
    counts = jnp.sum(present.astype(jnp.int32), axis=1)
    return counts.astype(jnp.int32), entries.astype(jnp.int32)


def solution(mesh):
    depth, terms = mesh.shape["rep"], mesh.shape["term"]

    def by_hand(panel_values, panel_ids, rows, cols, blocks):
        panels_each, _, passages, size = panel_values.shape
        tiles, total, entries = gather_by_hand(
            panel_ids.reshape(panels_each), rows, cols, panel_values.reshape(panels_each * passages, size), blocks
        )
        return held_products(tiles, total, entries, blocks)

    def local(panel_values, panel_ids, block_rows, block_cols):
        panels_each, own_slots, passages, size = panel_values.shape
        blocks = block_rows.shape[0] // depth
        slots = terms * own_slots
        shaped = own_slots == 1 and panels_each == EACH and passages == size == LANES
        if terms == CORES * SIDE * SIDE and depth == DEPTH and shaped and 2 * blocks + LATE_BATCH < LANES and blocks % 8 == 0:
            return by_hand(panel_values, panel_ids, block_rows, block_cols, blocks)
        first = lax.axis_index("rep") * blocks
        rows = lax.dynamic_slice_in_dim(block_rows, first, blocks)
        cols = lax.dynamic_slice_in_dim(block_cols, first, blocks)
        shard = jnp.swapaxes(panel_values, 0, 1).reshape(own_slots, panels_each * passages, size)
        tiles = lax.all_gather(shard, ("rep", "term"), axis=0, tiled=True)
        tiles = tiles.reshape(depth, slots, panels_each * passages, size)
        ids = lax.all_gather(panel_ids.T, ("rep", "term"), axis=0, tiled=True)
        ids = ids.reshape(depth, slots, panels_each)
        ids = jnp.swapaxes(ids, 1, 2).reshape(depth * panels_each, slots)
        counts, entries = block_list(ids, rows, cols)
        return products(tiles, slots, panels_each, counts, entries, blocks)

    placed = (P("rep", "term", None, None), P("rep", "term"), P("term"), P("term"))
    return jax.shard_map(
        local, mesh=mesh, in_specs=placed, out_specs=P(("term", "rep"), None, None), check_vma=False
    )
```

```python
import functools

import jax
import jax.numpy as jnp
from jax import lax
from jax.experimental import pallas as pl
from jax.experimental.pallas import tpu as pltpu
from jax.sharding import PartitionSpec as P

MESH = pl.DeviceIdType.MESH
CORES = 2
SIDE = 2
ROWS = 8
LANES = 128
DEPTH = 4
EACH = 4
UNROLL = 6
WINDOW = 2
LEVELS = {True: (0, 1, 2, 3), False: (1, 0, 2, 3)}
PAIRS = DEPTH * EACH // 2
KEPT = 30
WORKS = 4
BATCH = 15
LATE_BATCH = 14
T_LINK, T_HOP, T_CROSS, T_OP = 1.43, 2.3, 0.9, 0.075
T_SETUP, T_PREPARE, T_PRODUCTS, T_COLLECT = 1.0, 0.8, 0.55, 0.55
X, Y, C, IN, OUT = range(5)
FLIP_X = {"S": "X", "X": "S", "Y": "D", "D": "Y"}
FLIP_Y = {"S": "Y", "Y": "S", "X": "D", "D": "X"}
COLUMNS = ("S", "X", "Y", "D")


def link_orders(end):
    own, every = (0, range(EACH)) if end else (1, range(EACH))
    whole = lambda column, level: [(column, level, j) for j in every]

    def crossing(levels, rest, odd, other):
        order = []
        for level in levels:
            order += [(other, level, odd), (other, level, 2 + odd)]
            order += [("S", level, j + 1 - odd - 2 * (j % 2) * (1 - odd)) for j in every]
        for level in rest:
            order += whole("S", level)
        return order

    if end:
        return {
            X: crossing((0, 1), (2, 3), 0, "Y"),
            Y: crossing((0, 1), (2, 3), 1, "X"),
            IN: whole("S", 0) + whole("D", 0),
        }
    return {
        X: crossing((1,), (0, 2, 3), 0, "Y"),
        Y: crossing((1,), (0, 2, 3), 1, "X"),
        IN: whole("S", 1) + whole("D", 1) + whole("S", 0) + whole("D", 0),
        OUT: whole("S", 1) + whole("S", 2) + whole("D", 2) + whole("S", 3) + whole("D", 3),
    }


RECEIVERS = {
    (True, X): (True, lambda c: (FLIP_X[c[0]], c[1], c[2])),
    (True, Y): (True, lambda c: (FLIP_Y[c[0]], c[1], c[2])),
    (True, IN): (False, lambda c: c),
    (False, X): (False, lambda c: (FLIP_X[c[0]], c[1], c[2])),
    (False, Y): (False, lambda c: (FLIP_Y[c[0]], c[1], c[2])),
    (False, IN): (False, lambda c: (c[0], DEPTH - 1 - c[1], c[2])),
    (False, OUT): (True, lambda c: c),
}


def final_items(end):
    passed = {chunk[:2] for order in link_orders(end).values() for chunk in order}
    return {(column, level) for column in COLUMNS for level in range(DEPTH)} - passed


def play_orders():
    orders = {end: link_orders(end) for end in (True, False)}
    into = RECEIVERS
    works = {}
    for end in (True, False):
        pairs = [(level, half) for level in LEVELS[end] for half in range(EACH // 2)][: PAIRS - 1]
        works[end] = [(T_SETUP, [])]
        for level, half in pairs:
            needed = [(column, level, half) for column in COLUMNS]
            works[end] += [(T_PREPARE, needed), (T_PRODUCTS, []), (T_PRODUCTS, []), (T_COLLECT, [])]
    final = {end: final_items(end) for end in (True, False)}
    clock = {True: 0.0, False: 0.0}
    have = {end: {("S", 0 if end else 1, j) for j in range(EACH)} for end in (True, False)}
    coming = {True: [], False: []}
    across = {True: {}, False: {}}
    crossed = {True: set(), False: set()}
    flight = {key: [] for key in into}
    sent = {key: set() for key in into}
    free = {key: 0.0 for key in into}
    worked = {True: 0, False: 0}
    ops = {True: [], False: []}

    def cross(end, column, level, half):
        ops[end].append(("cross", None, (column, level, half)))
        across[end][column, level, half] = clock[end] + T_CROSS

    def act(end):
        now = clock[end]
        for arrival in sorted(coming[end]):
            if arrival[0] <= now:
                column, level, j = arrival[1]
                coming[end].remove(arrival)
                if (column, level) in final[end] and (column, level, j ^ 1) not in have[end]:
                    have[end].add(arrival[1])
                    return 0.0
                have[end].add(arrival[1])
                ops[end].append(("take", None, arrival[1]))
                if (column, level, j ^ 1) in have[end]:
                    cross(end, column, level, j // 2)
                return T_OP
        for way, order in orders[end].items():
            key = (end, way)
            while flight[key] and flight[key][0] <= now:
                flight[key].pop(0)
            ready = [chunk for chunk in order if chunk in have[end] and chunk not in sent[key]]
            if ready and len(flight[key]) < WINDOW:
                chunk = ready[0]
                ops[end].append(("start", way, chunk))
                sent[key].add(chunk)
                free[key] = max(free[key], now) + T_LINK
                flight[key].append(free[key])
                receiver, rename = into[key]
                coming[receiver].append((free[key] + T_HOP, rename(chunk)))
                return T_OP
        if worked[end] < len(works[end]):
            lasts, needed = works[end][worked[end]]
            if all(across[end].get(c, now + 1) <= now for c in needed):
                ops[end] += [("across", None, c) for c in needed]
                crossed[end].update(needed)
                ops[end].append(("work", None, None))
                worked[end] += 1
                return lasts
        return None

    for end in (True, False):
        for half in range(EACH // 2):
            cross(end, "S", 0 if end else 1, half)
    while True:
        end = clock[True] <= clock[False]
        spent = act(end)
        if spent is not None:
            clock[end] += spent
            continue
        later = [t for t, _ in coming[end]] + list(across[end].values())
        later += [held[0] for (kind, _), held in flight.items() if kind == end and held]
        later = [t for t in later if t > clock[end]]
        other = clock[not end]
        if not later and act(not end) is None and not [t for t, _ in coming[not end] if t > other]:
            break
        clock[end] = min(later + [max(other, clock[end]) + T_OP])
    for end in (True, False):
        every = [(column, level, half) for column in COLUMNS for level in range(DEPTH) for half in range(EACH // 2)]
        ops[end] += [("across", None, c) for c in every if c not in crossed[end]]
        for way, order in orders[end].items():
            items = dict.fromkeys((chunk[0], chunk[1]) for chunk in order)
            for whole in (True, False):
                number = sum((column == "S" or way in (IN, OUT)) == whole for column, _ in items)
                if number:
                    ops[end].append(("settle", way, (number, whole, 0 if whole or way == X else 1)))
        ops[end].append(("settle", C, (len(COLUMNS) * DEPTH, True, 0)))
    return ops, clock


def gather_kernel(
    blocks, ids_hbm, rows_hbm, cols_hbm, shard_ref, tiles_ref, total_ref, list_ref, ids_in, rows_in, cols_in,
    made_ref, left_ref, right_ref, table_ref, index_ref,
    small_sem, own_sem, table_sem, send_sem, recv_sem, cross_sem,
):
    term = lax.axis_index("term")
    z = lax.axis_index("rep")
    core = term % CORES
    x = (term // CORES) % SIDE
    y = term // (CORES * SIDE)
    terms = CORES * SIDE * SIDE
    upper = (z >= DEPTH // 2).astype(jnp.int32)
    at_end = (z == 0) | (z == DEPTH - 1)
    inner = jnp.logical_not(at_end)
    inward = 1 - 2 * upper
    size = shard_ref.shape[1]

    def term_of(column, at_core):
        at_x = 1 - x if column in ("X", "D") else x
        at_y = 1 - y if column in ("Y", "D") else y
        return (at_y * SIDE + at_x) * CORES + at_core

    def level_of(level):
        return level + upper * (DEPTH - 1 - 2 * level)

    def slot_of(column, level, at_core):
        return level_of(level) * terms + term_of(column, at_core)

    target = {
        X: (term_of("X", core), z),
        Y: (term_of("Y", core), z),
        C: (term_of("S", 1 - core), z),
        IN: (term, z + inward),
        OUT: (term, z - inward),
    }
    smalls = [
        pltpu.make_async_copy(source, held, small_sem.at[i])
        for i, (source, held) in enumerate(((ids_hbm, ids_in), (rows_hbm, rows_in), (cols_hbm, cols_in)))
    ]
    for small in smalls:
        small.start()
    barrier = pltpu.get_barrier_semaphore()

    def greet(way):
        pl.semaphore_signal(barrier, inc=1, device_id=target[way], device_id_type=MESH)

    for way in (X, Y, C, IN):
        greet(way)
    pl.when(inner)(lambda: greet(OUT))
    own_slot = z * terms + term
    own = pltpu.make_async_copy(shard_ref, tiles_ref.at[own_slot, pl.ds(ROWS, EACH * size)], own_sem)
    own.start()
    sub = lax.broadcasted_iota(jnp.int32, (ROWS, LANES), 0)
    lane = lax.broadcasted_iota(jnp.int32, (ROWS, LANES), 1)
    ids = jnp.full((ROWS, LANES), -1, jnp.int32)
    for small in smalls:
        small.wait()
    for j in range(EACH):
        ids = jnp.where(sub == j, ids_in[j], ids)
    tiles_ref[own_slot, :ROWS] = ids.astype(jnp.float32)
    own.wait()
    pl.semaphore_wait(barrier, 4 + inner.astype(jnp.int32))

    def rows_of(j, width=1):
        return pl.ds(0, ROWS + width * size) if j == 0 else pl.ds(ROWS + j * size, width * size)

    final = {end: final_items(end) for end in (True, False)}

    def copy(end, way, column, level, j, width):
        mark = j
        if way != C:
            receiver, rename = RECEIVERS[end, way]
            if rename((column, level, j))[:2] in final[receiver]:
                mark = j & 2
        slot = slot_of(column, level, core)
        part = tiles_ref.at[slot, rows_of(j, width)]
        return pltpu.make_async_remote_copy(
            src_ref=part, dst_ref=part, send_sem=send_sem.at[way, int(way in (X, Y) and column != "S")],
            recv_sem=cross_sem.at[slot, j // 2] if way == C else recv_sem.at[slot, mark],
            device_id=target[way], device_id_type=MESH,
        )

    def landed(slot, rows, sem):
        part = tiles_ref.at[slot, rows]
        pltpu.make_async_remote_copy(
            src_ref=part, dst_ref=part, send_sem=send_sem.at[0, 0], recv_sem=sem,
            device_id=target[C], device_id_type=MESH,
        ).wait_recv()

    def left(way, number, whole, odd):
        rows = (EACH if whole else 2) * size + (0 if odd else ROWS)
        part = tiles_ref.at[pl.ds(0, number), pl.ds(0, rows)]
        pltpu.make_async_remote_copy(
            src_ref=part, dst_ref=part, send_sem=send_sem.at[way, int(not whole)], recv_sem=recv_sem.at[0, 0],
            device_id=target[way], device_id_type=MESH,
        ).wait_send()

    ops, _ = play_orders()
    groups = {}
    for end in (True, False):
        groups[end] = [[]]
        for op in ops[end]:
            if op[0] == "work":
                groups[end].append([])
            else:
                groups[end][-1].append(op)

    def play(end, index):
        for name, way, (column, level, j) in groups[end][index]:
            if name == "take":
                slot = slot_of(column, level, core)
                if (column, level) in final[end]:
                    landed(slot, rows_of(j & 2, 2), recv_sem.at[slot, j & 2])
                else:
                    landed(slot, rows_of(j), recv_sem.at[slot, j])
            elif name == "across":
                slot = slot_of(column, level, 1 - core)
                landed(slot, rows_of(2 * j, 2), cross_sem.at[slot, j])
            elif name == "start":
                copy(end, way, column, level, j, 1).start()
            elif name == "cross":
                copy(end, C, column, level, 2 * j, 2).start()
            else:
                left(way, column, level, j)

    def both_kinds(act):
        lax.cond(at_end, lambda: act(True), lambda: act(False))

    halves = EACH // 2

    both_kinds(lambda end: play(end, 0))

    wanted_row = jnp.full((ROWS, LANES), -2, jnp.int32)
    wanted_col = wanted_row
    for b in range(blocks):
        wanted_row = jnp.where(lane == b, rows_in[z * blocks + b], wanted_row)
        wanted_col = jnp.where(lane == b, cols_in[z * blocks + b], wanted_col)
    table_ref[0] = wanted_row
    table_ref[1] = wanted_col

    def clear_total(b, _):
        total_ref[b] = jnp.zeros((size, size), jnp.float32)
        return 0

    lax.fori_loop(0, blocks, clear_total, 0)
    made_ref[KEPT] = jnp.zeros((size, size), jnp.float32)
    before = (
        lax.broadcasted_iota(jnp.int32, (LANES, LANES), 0) < lax.broadcasted_iota(jnp.int32, (LANES, LANES), 1)
    ).astype(jnp.float32)

    table_copy = pltpu.make_async_copy(table_ref.at[pl.ds(2, 2)], index_ref, table_sem)

    def make_table(level):
        want_row, want_col = table_ref[0].astype(jnp.float32), table_ref[1].astype(jnp.float32)
        slot_row = jnp.full((ROWS, LANES), -1, jnp.int32)
        slot_col = slot_row
        for t in range(terms):
            listed = tiles_ref[level * terms + t, :ROWS]
            slot_row = jnp.where(listed == want_row, t, slot_row)
            slot_col = jnp.where(listed == want_col, t, slot_col)
        present = (slot_row >= 0) & (slot_col >= 0)
        ones = jnp.where(present, 1.0, 0.0).astype(jnp.float32)
        ahead = jnp.dot(ones, before, preferred_element_type=jnp.float32)
        count = jnp.sum(ones, axis=1, keepdims=True)
        twin = jnp.concatenate([count[:1] * 0.0, count[: ROWS - 1]], axis=0)
        ahead = ahead + jnp.where(sub % 2 == 1, twin, 0.0)
        place = jnp.clip(jnp.where(present, ahead, float(LANES)).astype(jnp.int32), 0, LANES)
        table_ref[3] = jnp.minimum(place, KEPT)
        upper_part = jnp.where(present, lane * 2 + sub % 2, 0).astype(jnp.float32)
        lower_part = jnp.where(present, slot_row * terms + slot_col, 0).astype(jnp.float32)
        parts = [
            jnp.concatenate([jnp.where(sub == j, part, 0.0) for j in range(EACH)], axis=1)
            for part in (upper_part, lower_part)
        ]
        deep = lax.broadcasted_iota(jnp.int32, (LANES, LANES), 0)
        chosen = jnp.concatenate(
            [jnp.where(place[j : j + 1] == deep, 1.0, 0.0).astype(jnp.bfloat16) for j in range(EACH)], axis=1
        )
        found = lax.dot_general(
            jnp.concatenate(parts, axis=0).astype(jnp.bfloat16), chosen, (((1,), (1,)), ((), ())),
            preferred_element_type=jnp.float32,
        )
        codes = found[:ROWS] * float(terms * terms) + found[ROWS:]
        codes = jnp.clip(codes.astype(jnp.int32), 0, 2 * blocks * terms * terms)
        entries = jnp.where(lane == LANES - 1, count.astype(jnp.int32), codes)
        table_ref[2] = entries
        for half in range(halves):
            both = entries[2 * half : 2 * half + 1] + entries[2 * half + 1 : 2 * half + 2]
            table_ref[2, half : half + 1] = both
            list_ref[pl.ds(level * halves + half, 1)] = both
        table_copy.start()

    def products(half, first):
        picked = [index_ref[0, half, first + k] for k in range(BATCH)]
        values = []
        for code in picked:
            pair = code % (2 * terms * terms)
            left = (pair // (terms * terms)) * terms + (pair // terms) % terms
            right = (pair // (terms * terms)) * terms + pair % terms
            values.append(jnp.dot(left_ref[left], right_ref[right], preferred_element_type=jnp.float32))
        for k, value in enumerate(values):
            made_ref[first + k] = value

    def collect(half):
        def one(b, _):
            j = half * 2
            total_ref[b] = total_ref[b] + (made_ref[index_ref[1, j, b]] + made_ref[index_ref[1, j + 1, b]])
            return 0

        lax.fori_loop(0, blocks, one, 0, unroll=8)

    def transfers(k, step):
        def choose(first, end_of):
            if end_of - first == 1:
                both_kinds(lambda end: play(end, first * WORKS + step + 1))
                return
            middle = (first + end_of) // 2
            lax.cond(k < middle, lambda: choose(first, middle), lambda: choose(middle, end_of))

        choose(0, PAIRS - 1)

    def pair(k, _):
        half = k % halves
        near = k // halves
        level = level_of(jnp.where(at_end | (near >= 2), near, 1 - near))
        transfers(k, 0)
        pl.when(half == 0)(lambda: make_table(level))
        for j in range(2):
            row = pl.multiple_of(ROWS + (half * 2 + j) * size, ROWS)
            for t in range(terms):
                prepare(tiles_ref[level * terms + t, pl.ds(row, size)], j * terms + t, left_ref, right_ref)
        pl.when(half == 0)(lambda: table_copy.wait())
        transfers(k, 1)
        products(half, 0)
        transfers(k, 2)
        products(half, BATCH)
        transfers(k, 3)
        collect(half)
        return 0

    lax.fori_loop(0, PAIRS - 1, pair, 0)
    both_kinds(lambda end: play(end, (PAIRS - 1) * WORKS + 1))


def gather_by_hand(ids, rows, cols, shard, blocks):
    terms = CORES * SIDE * SIDE
    size = shard.shape[1]
    vmem = pl.BlockSpec(memory_space=pltpu.VMEM)
    return pl.pallas_call(
        functools.partial(gather_kernel, blocks),
        out_shape=(
            pltpu.VMEM((DEPTH * terms, ROWS + shard.shape[0], size), jnp.float32),
            pltpu.VMEM((blocks + 1, size, size), jnp.float32),
            pltpu.VMEM((ROWS, LANES), jnp.int32),
        ),
        in_specs=[pl.BlockSpec(memory_space=pltpu.HBM)] * 4,
        out_specs=(vmem, vmem, vmem),
        scratch_shapes=[
            pltpu.SMEM(ids.shape, jnp.int32),
            pltpu.SMEM(rows.shape, jnp.int32),
            pltpu.SMEM(cols.shape, jnp.int32),
            pltpu.VMEM((KEPT + 1, size, size), jnp.float32),
            pltpu.VMEM((2 * terms, size, 3 * size), jnp.bfloat16),
            pltpu.VMEM((2 * terms, 3 * size, size), jnp.bfloat16),
            pltpu.VMEM((4, ROWS, LANES), jnp.int32),
            pltpu.SMEM((2, ROWS, LANES), jnp.int32),
            pltpu.SemaphoreType.DMA((3,)),
            pltpu.SemaphoreType.DMA,
            pltpu.SemaphoreType.DMA,
            pltpu.SemaphoreType.DMA((5, 2)),
            pltpu.SemaphoreType.DMA((DEPTH * terms, EACH)),
            pltpu.SemaphoreType.DMA((DEPTH * terms, EACH // 2)),
        ],
        compiler_params=pltpu.CompilerParams(
            collective_id=0, has_side_effects=True, vmem_limit_bytes=30 * 1024 * 1024
        ),
    )(*(pltpu.with_memory_space_constraint(value, pltpu.HBM) for value in (ids, rows, cols, shard)))


def split(value):
    high = value.astype(jnp.bfloat16)
    return high, (value - high.astype(jnp.float32)).astype(jnp.bfloat16)


def prepare(value, s, left_ref, right_ref):
    size = value.shape[0]
    high, low = split(value)
    right_ref[s, :size] = high
    right_ref[s, size : 2 * size] = high
    right_ref[s, 2 * size :] = low
    high, low = split(value.T)
    left_ref[s, :, :size] = high
    left_ref[s, :, size : 2 * size] = low
    left_ref[s, :, 2 * size :] = high


def add_products(slots, read, count, out_ref, left_ref, right_ref, filled):
    def entries(first, width):
        picked = []
        for k in range(width):
            code = read(first + k)
            pair = code % (slots * slots)
            picked.append((code // (slots * slots), pair // slots, pair % slots))
        sums = [
            out_ref[b] + jnp.dot(left_ref[r], right_ref[c], preferred_element_type=jnp.float32)
            for b, r, c in picked
        ]
        for (b, _, _), value in zip(picked, sums):
            out_ref[b] = value

    groups = (count + UNROLL - 1) // UNROLL if filled else count // UNROLL
    pl.loop(0, groups)(lambda i: entries(i * UNROLL, UNROLL))
    if filled:
        return
    pl.loop(groups * UNROLL, count)(lambda i: entries(i, 1))


def clear(out_ref):
    def one(b, _):
        out_ref[b] = jnp.zeros(out_ref.shape[1:], jnp.float32)
        return 0

    lax.fori_loop(0, out_ref.shape[0], one, 0)


def held_kernel(blocks, tiles_ref, total_in, list_in, out_ref, total_ref, left_ref, right_ref, list_ref, list_sem, out_sem):
    terms = CORES * SIDE * SIDE
    size = tiles_ref.shape[2]
    z = lax.axis_index("rep")
    fetch = pltpu.make_async_copy(list_in, list_ref, list_sem)
    fetch.start()

    def get_ready(place):
        slot = place // 2 * terms
        for j in range(2):
            row = pl.multiple_of(ROWS + (place % 2 * 2 + j) * size, ROWS)
            for s in range(terms):
                prepare(tiles_ref[slot + s, pl.ds(row, size)], j * terms + s, left_ref, right_ref)

    def add(place, first, width):
        values = []
        for k in range(width):
            code = list_ref[place, first + k]
            pair = code % (2 * terms * terms)
            left = (pair // (terms * terms)) * terms + (pair // terms) % terms
            right = (pair // (terms * terms)) * terms + pair % terms
            value = jnp.dot(left_ref[left], right_ref[right], preferred_element_type=jnp.float32)
            values.append((jnp.where(first + k < list_ref[place, LANES - 1], code // (2 * terms * terms), blocks), value))
        for b, value in values:
            total_ref[b] = total_ref[b] + value

    def add_from(place, first):
        groups = (list_ref[place, LANES - 1] - first + LATE_BATCH - 1) // LATE_BATCH
        pl.loop(0, groups)(lambda i: add(place, first + i * LATE_BATCH, LATE_BATCH))

    last = jnp.where(z >= DEPTH // 2, 1, PAIRS - 1)
    get_ready(last)
    fetch.wait()
    add_from(last, 0)

    def rest(place):
        def more():
            get_ready(place)
            add_from(place, KEPT)

        pl.when((place != last) & (list_ref[place, LANES - 1] > KEPT))(more)

    pl.loop(0, PAIRS)(rest)
    pieces = out_sem.shape[0]
    each = blocks // pieces
    outs = [
        pltpu.make_async_copy(total_ref.at[pl.ds(i * each, each)], out_ref.at[pl.ds(i * each, each)], out_sem.at[i])
        for i in range(pieces)
    ]
    for out in outs:
        out.start()
    for out in outs:
        out.wait()


def held_products(tiles, total, entries, blocks):
    size = tiles.shape[2]
    terms = CORES * SIDE * SIDE
    pieces = next(n for n in (8, 7, 4, 2, 1) if blocks % n == 0)
    vmem = pl.BlockSpec(memory_space=pltpu.VMEM)
    return pl.pallas_call(
        functools.partial(held_kernel, blocks),
        out_shape=(
            jax.ShapeDtypeStruct((blocks, size, size), jnp.float32),
            pltpu.VMEM(total.shape, jnp.float32),
        ),
        in_specs=[vmem, vmem, vmem],
        out_specs=(pl.BlockSpec(memory_space=pl.ANY), vmem),
        input_output_aliases={1: 1},
        scratch_shapes=[
            pltpu.VMEM((2 * terms, size, 3 * size), jnp.bfloat16),
            pltpu.VMEM((2 * terms, 3 * size, size), jnp.bfloat16),
            pltpu.SMEM((ROWS, LANES), jnp.int32),
            pltpu.SemaphoreType.DMA,
            pltpu.SemaphoreType.DMA((pieces,)),
        ],
        compiler_params=pltpu.CompilerParams(vmem_limit_bytes=16 * 1024 * 1024),
    )(tiles, total, entries)[0]


def product_kernel(slots, base, count_ref, list_ref, tiles_ref, out_ref, left_ref, right_ref):
    panel = pl.program_id(0)

    pl.when(panel == 0)(lambda: clear(out_ref))
    pl.loop(0, slots)(lambda s: prepare(tiles_ref[0, s], s, left_ref, right_ref))
    add_products(
        slots, lambda k: list_ref[panel * base + k], count_ref[panel], out_ref, left_ref, right_ref, False
    )


def products(tiles, slots, panels_each, counts, entries, blocks):
    groups, size = tiles.shape[0], tiles.shape[3]
    return pl.pallas_call(
        functools.partial(product_kernel, slots, entries.shape[1]),
        out_shape=jax.ShapeDtypeStruct((blocks, size, size), jnp.float32),
        grid_spec=pltpu.PrefetchScalarGridSpec(
            num_scalar_prefetch=2,
            grid=(groups * panels_each,),
            in_specs=[
                pl.BlockSpec(
                    (1, slots, size, size), lambda p, *_: (p // panels_each, 0, p % panels_each, 0)
                )
            ],
            out_specs=pl.BlockSpec((blocks, size, size), lambda p, *_: (0, 0, 0)),
            scratch_shapes=[
                pltpu.VMEM((slots, size, 3 * size), jnp.bfloat16),
                pltpu.VMEM((slots, 3 * size, size), jnp.bfloat16),
            ],
        ),
        compiler_params=pltpu.CompilerParams(
            dimension_semantics=("arbitrary",), vmem_limit_bytes=56 * 1024 * 1024
        ),
    )(counts, entries.reshape(-1), tiles)


def block_list(ids, rows, cols):
    slots, blocks = ids.shape[1], rows.shape[0]
    order = jnp.arange(slots, dtype=jnp.int32)[None, :, None]
    match_row = ids[:, :, None] == rows[None, None, :]
    match_col = ids[:, :, None] == cols[None, None, :]
    slot_row = jnp.sum(jnp.where(match_row, order, 0), axis=1)
    slot_col = jnp.sum(jnp.where(match_col, order, 0), axis=1)
    present = jnp.any(match_row, axis=1) & jnp.any(match_col, axis=1)
    number = jnp.arange(blocks, dtype=jnp.int32)
    code = (number[None, :] * slots + slot_row) * slots + slot_col
    ahead = jnp.sum(
        jnp.where(present[:, None, :] & (number[None, None, :] < number[None, :, None]), 1, 0), axis=2
    )
    chosen = present[:, None, :] & (ahead[:, None, :] == number[None, :, None])
    entries = jnp.sum(jnp.where(chosen, code[:, None, :], 0), axis=2)
    counts = jnp.sum(present.astype(jnp.int32), axis=1)
    return counts.astype(jnp.int32), entries.astype(jnp.int32)


def solution(mesh):
    depth, terms = mesh.shape["rep"], mesh.shape["term"]

    def by_hand(panel_values, panel_ids, rows, cols, blocks):
        panels_each, _, passages, size = panel_values.shape
        tiles, total, entries = gather_by_hand(
            panel_ids.reshape(panels_each), rows, cols, panel_values.reshape(panels_each * passages, size), blocks
        )
        return held_products(tiles, total, entries, blocks)

    def local(panel_values, panel_ids, block_rows, block_cols):
        panels_each, own_slots, passages, size = panel_values.shape
        blocks = block_rows.shape[0] // depth
        slots = terms * own_slots
        shaped = own_slots == 1 and panels_each == EACH and passages == size == LANES
        if terms == CORES * SIDE * SIDE and depth == DEPTH and shaped and 2 * blocks + LATE_BATCH < LANES and blocks % 8 == 0:
            return by_hand(panel_values, panel_ids, block_rows, block_cols, blocks)
        first = lax.axis_index("rep") * blocks
        rows = lax.dynamic_slice_in_dim(block_rows, first, blocks)
        cols = lax.dynamic_slice_in_dim(block_cols, first, blocks)
        shard = jnp.swapaxes(panel_values, 0, 1).reshape(own_slots, panels_each * passages, size)
        tiles = lax.all_gather(shard, ("rep", "term"), axis=0, tiled=True)
        tiles = tiles.reshape(depth, slots, panels_each * passages, size)
        ids = lax.all_gather(panel_ids.T, ("rep", "term"), axis=0, tiled=True)
        ids = ids.reshape(depth, slots, panels_each)
        ids = jnp.swapaxes(ids, 1, 2).reshape(depth * panels_each, slots)
        counts, entries = block_list(ids, rows, cols)
        return products(tiles, slots, panels_each, counts, entries, blocks)

    placed = (P("rep", "term", None, None), P("rep", "term"), P("term"), P("term"))
    return jax.shard_map(
        local, mesh=mesh, in_specs=placed, out_specs=P(("term", "rep"), None, None), check_vma=False
    )
```
